128 devices in a mesh: fsdp: 128 (over y, z, x, core).
Axes of the slice: x: 4, y: 4, z: 4, core: 2. Of those that a mesh axis runs over, the one named last changes fastest.
Arguments:
- hidden_in: bfloat16 [16384, 1024], P('fsdp'), may hold values from -24 to 24
- norm1_gain: bfloat16 [1024], P('fsdp'), may hold values from 0.099609375 to 1.8984375
- in_weight: bfloat16 [1024, 3072], P('fsdp'), may hold values from -0.1875 to 0.1875
- conv_weight: bfloat16 [1024, 3], P('fsdp'), may hold values from -3 to 3
- out_weight: bfloat16 [1024, 1024], P('fsdp'), may hold values from -0.1875 to 0.1875
- norm2_gain: bfloat16 [1024], P('fsdp'), may hold values from 0.099609375 to 1.8984375
- gate_weight: bfloat16 [1024, 4608], P('fsdp'), may hold values from -0.1875 to 0.1875
- up_weight: bfloat16 [1024, 4608], P('fsdp'), may hold values from -0.1875 to 0.1875
- down_weight: bfloat16 [4608, 1024], P('fsdp'), may hold values from -0.125 to 0.125
- segment_ids: int32 [16384], P('fsdp'), may hold values from 0 to 63, never falling along the last dimension, each value on 1 to 512 neighbouring positions
- cotangent: bfloat16 [16384, 1024], P('fsdp'), may hold values from -6 to 6
Outputs:
- block_out: bfloat16 [16384, 1024], P('fsdp')
- input_grad: float32 [16384, 1024], P('fsdp')
- norm1_gain_grad: float32 [1024], P('fsdp')
- in_weight_grad: float32 [1024, 3072], P('fsdp')
- conv_weight_grad: float32 [1024, 3], P('fsdp')
- out_weight_grad: float32 [1024, 1024], P('fsdp')
- norm2_gain_grad: float32 [1024], P('fsdp')
- gate_weight_grad: float32 [1024, 4608], P('fsdp')
- up_weight_grad: float32 [1024, 4608], P('fsdp')
- down_weight_grad: float32 [4608, 1024], P('fsdp')
The draws below stay inside these ranges and needn't reach their ends.
Inputs may be any that keep to these rules, and one draw needn't show every extreme that they name: `segment_ids`: document numbers never fall along the tokens; each document covers 1 to 512 tokens, one exactly 512.
All inputs are finite; a program needn't handle non-finite values.
Results may differ from the reference program's by a relative error of at most 0.011.
Values may be sent and summed in bfloat16 or wider, within the bound.
A program may use at most 192 MiB of HBM per device.

```python
import math
import jax
import jax.numpy as jnp
import numpy as np
from jax import lax

D = 1024
FF = 4608
CONV = 3
TOKENS = 16384
DOC_MOST = 512
SEGS = 64


def spiked(values, stream_key, source, target, shards_of, factor):
    def block_of(axis_at):
        return (jnp.arange(values.shape[axis_at]) // (values.shape[axis_at] // shards_of)).reshape((-1,) + (1,) * (values.ndim - 1 - axis_at))

    one_side = jax.random.permutation(stream_key, shards_of)[block_of(target)]
    far = (block_of(target) + shards_of // 2) % shards_of
    return jnp.where((block_of(source) == one_side) | (block_of(source) == far), factor * values, values)


def levels(own_key, extent, split, least, top_value):
    def one(dim, parts):
        heights = jax.random.uniform(jax.random.fold_in(jax.random.fold_in(own_key, 6), dim), (parts,), jnp.float32, least / len(split), top_value / len(split))
        return jnp.repeat(jnp.exp(heights), extent[dim] // parts).reshape((-1,) + (1,) * (len(extent) - dim - 1))

    level = one(*split[0])
    for cut in split[1:]:
        level = level * one(*cut)
    return level


def split_up(count, total, reach, skew):
    loads = [(1 << 20) // math.isqrt(standing ** skew) + 1 for standing in range(2, count + 1)]
    rest, holding = total - reach - (count - 1), [1] * (count - 1)
    while rest > 0:
        candidates = [i for i in range(count - 1) if holding[i] < reach]
        whole, budget = sum([loads[i] for i in candidates]), rest
        for i in candidates:
            extra = min(reach - holding[i], max(1, budget * loads[i] // whole), rest)
            holding[i] = holding[i] + extra
            rest = rest - extra
    return np.array([reach] + holding)


def ragged(stream_key, amount, total, reach, lean):
    if amount == 2:
        one = jax.random.randint(stream_key, (), max(1, total - reach), min(reach, total - 1) + 1)
        return jnp.stack([one, total - one])
    lengths = jnp.asarray(split_up(amount, total, reach, lean), jnp.int32)
    pairs = (amount - 1) // 2
    source_of, sink = lengths[1:1 + 2 * pairs:2], lengths[2:2 + 2 * pairs:2]
    slack = jnp.minimum(source_of - 1, reach - sink)
    shifted = jax.random.randint(jax.random.fold_in(stream_key, 1), (pairs,), 0, 1 << 20) % (slack + 1)
    lengths = lengths.at[1:1 + 2 * pairs:2].set(source_of - shifted).at[2:2 + 2 * pairs:2].set(sink + shifted)
    return lengths[jax.random.permutation(jax.random.fold_in(stream_key, 2), amount)]


def normal_values(stream_key, dims, deviation, reach, cuts=(), held_as=jnp.bfloat16):
    values = deviation * jax.random.normal(stream_key, dims, jnp.float32)
    if cuts:
        values = values * levels(stream_key, dims, cuts, -0.22, 0.18)
    return jnp.clip(values, -reach, reach).astype(held_as)


def gaussian_with(stream_key, shape, width, limit, shards, heavy, dtype=jnp.bfloat16):
    array = width * jax.random.normal(stream_key, shape, jnp.float32)
    if shards:
        array = array * levels(stream_key, shape, shards, -0.22, 0.18)
    return jnp.clip(spiked(array, jax.random.fold_in(stream_key, 3), *heavy), -limit, limit).astype(dtype)


def setup_inputs(seed: int = 0) -> dict:
    arg_keys = jax.random.split(jax.random.key(seed), 12)
    hidden_in = gaussian_with(arg_keys[0], (TOKENS, D), 1.0, 24.0, ((0, 128),), (0, 1, 128, 5.5))
    norm1_gain = jnp.clip(1.0 + 0.18 * jax.random.normal(arg_keys[1], (D,), jnp.float32), 0.099609375, 1.8984375).astype(jnp.bfloat16)
    in_weight = normal_values(arg_keys[2], (D, 3 * D), D ** -0.5, 0.1875, ((0, 128),))
    conv_weight = normal_values(arg_keys[3], (D, CONV), 0.6, 3.0, ((0, 128),))
    out_weight = normal_values(arg_keys[4], (D, D), D ** -0.5, 0.1875, ((0, 128),))
    norm2_gain = jnp.clip(1.0 + 0.18 * jax.random.normal(arg_keys[5], (D,), jnp.float32), 0.099609375, 1.8984375).astype(jnp.bfloat16)
    gate_weight = normal_values(arg_keys[6], (D, FF), D ** -0.5, 0.1875, ((0, 128),))
    up_weight = normal_values(arg_keys[7], (D, FF), D ** -0.5, 0.1875, ((0, 128),))
    down_weight = normal_values(arg_keys[8], (FF, D), (FF // 2) ** -0.5, 0.125, ((0, 128),))
    segment_ids = jnp.searchsorted(jnp.cumsum(ragged(arg_keys[9], SEGS, TOKENS, DOC_MOST, 0)), jnp.arange(TOKENS), side="right").astype(jnp.int32)
    cotangent = normal_values(arg_keys[10], (TOKENS, D), 1.0, 6.0, ((0, 128),))
    return {"hidden_in": hidden_in, "norm1_gain": norm1_gain, "in_weight": in_weight, "conv_weight": conv_weight, "out_weight": out_weight, "norm2_gain": norm2_gain, "gate_weight": gate_weight, "up_weight": up_weight, "down_weight": down_weight, "segment_ids": segment_ids, "cotangent": cotangent}


EPS = 1e-05

def rms_scale(values):
    return lax.rsqrt(lax.optimization_barrier(jnp.mean(values * values, axis=-1, keepdims=True)) + EPS)

def mixer_input(block_x, norm1_gain, in_weight):
    xf = block_x.astype(jnp.float32)
    s1 = rms_scale(xf)
    h = (xf * s1 * norm1_gain.astype(jnp.float32)).astype(jnp.bfloat16)
    proj = jnp.dot(h, in_weight, preferred_element_type=jnp.float32)
    return (xf, s1, h, proj[:, :D], proj[:, D:2 * D], proj[:, 2 * D:])

def extended(bx, segment_ids):
    ext_bx = jnp.concatenate([jnp.zeros((2, D), jnp.bfloat16), bx], axis=0).astype(jnp.float32)
    ext_ids = jnp.concatenate([jnp.full((2,), -1, jnp.int32), segment_ids.astype(jnp.int32)], axis=0)
    return (ext_bx, ext_ids)

def conv_forward(bx, segment_ids, conv_weight):
    count = bx.shape[0]
    ext_bx, ext_ids = extended(bx, segment_ids)
    weights = conv_weight.astype(jnp.float32)
    total = jnp.zeros((count, D), jnp.float32)
    for k in range(CONV):
        mask = (ext_ids[2 - k:2 - k + count] == segment_ids).astype(jnp.float32)[:, None]
        total = total + weights[:, k] * mask * ext_bx[2 - k:2 - k + count]
    return total

def conv_backward(du, bx, segment_ids, conv_weight):
    count = du.shape[0]
    ext_bx, ext_ids = extended(bx, segment_ids)
    weights = conv_weight.astype(jnp.float32)
    dext = jnp.zeros((count + 2, D), jnp.float32)
    columns = []
    for k in range(CONV):
        mask = (ext_ids[2 - k:2 - k + count] == segment_ids).astype(jnp.float32)[:, None]
        term = du * mask
        dext = dext + jnp.pad(weights[:, k] * term, ((2 - k, k), (0, 0)))
        columns.append(lax.optimization_barrier(jnp.sum(term * ext_bx[2 - k:2 - k + count], axis=0)))
    return (dext[2:], jnp.stack(columns, axis=1))

def reference(hidden_in, norm1_gain, in_weight, conv_weight, out_weight, norm2_gain, gate_weight, up_weight, down_weight, segment_ids, cotangent):
    block = math.gcd(TOKENS, 4096)
    count = TOKENS // block
    xs = hidden_in.reshape(count, block, D)
    cots = cotangent.reshape(count, block, D)

    def first(carry, block_x):
        xf, s1, h, bgate, cgate, xv = mixer_input(block_x, norm1_gain, in_weight)
        return (carry, (bgate * xv).astype(jnp.bfloat16))
    _, bx = lax.scan(first, jnp.zeros((), jnp.float32), xs)
    bx = bx.reshape(TOKENS, D)
    u = conv_forward(bx, segment_ids, conv_weight)
    us = u.reshape(count, block, D)
    gain2 = norm2_gain.astype(jnp.float32)

    def second(carry, inputs):
        block_x, block_u, cot = inputs
        xf, s1, h, bgate, cgate, xv = mixer_input(block_x, norm1_gain, in_weight)
        y = (cgate * block_u).astype(jnp.bfloat16)
        r = xf + jnp.dot(y, out_weight, preferred_element_type=jnp.float32)
        s2 = rms_scale(r)
        h2 = (r * s2 * gain2).astype(jnp.bfloat16)
        a = jnp.dot(h2, gate_weight, preferred_element_type=jnp.float32)
        b = jnp.dot(h2, up_weight, preferred_element_type=jnp.float32)
        sig = jax.nn.sigmoid(a)
        act = a * sig
        z = (act * b).astype(jnp.bfloat16)
        out = (r + jnp.dot(z, down_weight, preferred_element_type=jnp.float32)).astype(jnp.bfloat16)
        dz = jnp.dot(cot, down_weight.T, preferred_element_type=jnp.float32)
        da = (dz * b * sig * (1.0 + a * (1.0 - sig))).astype(jnp.bfloat16)
        db = (dz * act).astype(jnp.bfloat16)
        g_down = jnp.dot(z.T, cot, preferred_element_type=jnp.float32)
        g_gate = jnp.dot(h2.T, da, preferred_element_type=jnp.float32)
        g_up = jnp.dot(h2.T, db, preferred_element_type=jnp.float32)
        dh2 = jnp.dot(da, gate_weight.T, preferred_element_type=jnp.float32) + jnp.dot(db, up_weight.T, preferred_element_type=jnp.float32)
        g_gain2 = lax.optimization_barrier(jnp.sum(dh2 * r * s2, axis=0))
        dn2 = dh2 * gain2
        dr = cot.astype(jnp.float32) + s2 * dn2 - r * (s2 * s2 * s2) * lax.optimization_barrier(jnp.mean(dn2 * r, axis=-1, keepdims=True))
        do = dr.astype(jnp.bfloat16)
        g_out = jnp.dot(y.T, do, preferred_element_type=jnp.float32)
        dy = jnp.dot(do, out_weight.T, preferred_element_type=jnp.float32)
        acc_out, acc_gain2, acc_gate, acc_up, acc_down = carry
        carry = (acc_out + g_out, acc_gain2 + g_gain2, acc_gate + g_gate, acc_up + g_up, acc_down + g_down)
        return (carry, (out, dr, dy * block_u, dy * cgate))
    init = (jnp.zeros((D, D), jnp.float32), jnp.zeros((D,), jnp.float32), jnp.zeros((D, FF), jnp.float32), jnp.zeros((D, FF), jnp.float32), jnp.zeros((FF, D), jnp.float32))
    sums, (outs, drs, dcs, dus) = lax.scan(second, init, (xs, us, cots))
    g_out, g_gain2, g_gate, g_up, g_down = sums
    dbx, g_conv = conv_backward(dus.reshape(TOKENS, D), bx, segment_ids, conv_weight)
    gain1 = norm1_gain.astype(jnp.float32)

    def third(carry, inputs):
        block_x, block_dbx, block_dc, block_dr = inputs
        xf, s1, h, bgate, cgate, xv = mixer_input(block_x, norm1_gain, in_weight)
        dproj = jnp.concatenate([block_dbx * xv, block_dc, block_dbx * bgate], axis=1).astype(jnp.bfloat16)
        g_in = jnp.dot(h.T, dproj, preferred_element_type=jnp.float32)
        dh = jnp.dot(dproj, in_weight.T, preferred_element_type=jnp.float32)
        g_gain1 = lax.optimization_barrier(jnp.sum(dh * xf * s1, axis=0))
        dn1 = dh * gain1
        dx = block_dr + s1 * dn1 - xf * (s1 * s1 * s1) * lax.optimization_barrier(jnp.mean(dn1 * xf, axis=-1, keepdims=True))
        return ((carry[0] + g_in, carry[1] + g_gain1), dx)
    init3 = (jnp.zeros((D, 3 * D), jnp.float32), jnp.zeros((D,), jnp.float32))
    (g_in, g_gain1), dxs = lax.scan(third, init3, (xs, dbx.reshape(count, block, D), dcs, drs))
    return (outs.reshape(TOKENS, D), dxs.reshape(TOKENS, D), g_gain1, g_in, g_conv, g_out, g_gain2, g_gate, g_up, g_down)
```

```python
import jax
import jax.numpy as jnp
from jax import lax
from jax.sharding import PartitionSpec as P

CONV = 3
EPS = 1e-05
LANE = 256


def shifted(value, axis, by):
    size = lax.axis_size(axis)
    pairs = [(i, i + by) for i in range(size) if 0 <= i + by < size]
    return lax.ppermute(value, axis, pairs)


def rms_scale(values):
    return lax.rsqrt(jnp.mean(values * values, axis=-1, keepdims=True) + EPS)


def pad_cols(x):
    extra = (-x.shape[1]) % LANE
    return jnp.pad(x, ((0, 0), (0, extra))) if extra else x


def gather_packed(pieces):
    widths = [p.shape[1] for p in pieces]
    packed = jnp.concatenate(pieces, axis=1)
    full = lax.all_gather(packed, "fsdp", axis=0, tiled=True)
    out, at = [], 0
    for w in widths:
        out.append(full[:, at : at + w])
        at += w
    return out


def scatter_packed(pieces):
    widths = [p.shape[1] for p in pieces]
    packed = jnp.concatenate(pieces, axis=1)
    mine = lax.optimization_barrier(
        lax.psum_scatter(packed, "fsdp", scatter_dimension=0, tiled=True)
    )
    out, at = [], 0
    for w in widths:
        out.append(mine[:, at : at + w])
        at += w
    return out


def per_device(
    hidden_in,
    norm1_gain,
    in_weight,
    conv_weight,
    out_weight,
    norm2_gain,
    gate_weight,
    up_weight,
    down_weight,
    segment_ids,
    cotangent,
):
    rows = hidden_in.shape[0]
    width = hidden_in.shape[1]
    per = in_weight.shape[0]
    n = lax.axis_size("fsdp")
    down_rows = down_weight.shape[0]
    small = jnp.concatenate(
        [norm1_gain[:, None], norm2_gain[:, None], conv_weight], axis=1
    )
    n_small = small.shape[1]
    w_in, w_out, small_full = gather_packed([in_weight, out_weight, pad_cols(small)])
    w_gate, w_up, w_down_packed = gather_packed(
        [gate_weight, up_weight, down_weight.reshape(per, -1)]
    )
    w_down = w_down_packed.reshape(n * down_rows, width)
    gain1 = small_full[:, 0]
    gain2 = small_full[:, 1]
    w_conv = small_full[:, 2 : 2 + CONV]

    xf = hidden_in.astype(jnp.float32)
    s1 = rms_scale(xf)
    h = (xf * s1 * gain1.astype(jnp.float32)).astype(jnp.bfloat16)
    proj = jnp.dot(h, w_in, preferred_element_type=jnp.float32)
    bgate = proj[:, :width]
    cgate = proj[:, width : 2 * width]
    xv = proj[:, 2 * width :]
    bx = (bgate * xv).astype(jnp.bfloat16)
    prev_rows, prev_ids = shifted(
        (bx[rows - 2 :], segment_ids[rows - 2 :].astype(jnp.bfloat16)), "fsdp", 1
    )
    ext_bx = jnp.concatenate([prev_rows, bx], axis=0).astype(jnp.float32)
    ext_ids = jnp.concatenate([prev_ids.astype(jnp.int32), segment_ids], axis=0)
    taps = w_conv.astype(jnp.float32)
    masks = [
        (ext_ids[2 - k : 2 - k + rows] == segment_ids).astype(jnp.float32)[:, None]
        for k in range(CONV)
    ]
    conv_out = jnp.zeros((rows, width), jnp.float32)
    for k in range(CONV):
        conv_out = conv_out + taps[:, k] * masks[k] * ext_bx[2 - k : 2 - k + rows]
    y = (cgate * conv_out).astype(jnp.bfloat16)
    resid = xf + jnp.dot(y, w_out, preferred_element_type=jnp.float32)
    s2 = rms_scale(resid)
    gain2f = gain2.astype(jnp.float32)
    h2 = (resid * s2 * gain2f).astype(jnp.bfloat16)
    a = jnp.dot(h2, w_gate, preferred_element_type=jnp.float32)
    b = jnp.dot(h2, w_up, preferred_element_type=jnp.float32)
    sig = jax.nn.sigmoid(a)
    act = a * sig
    z = (act * b).astype(jnp.bfloat16)
    block_out = (resid + jnp.dot(z, w_down, preferred_element_type=jnp.float32)).astype(
        jnp.bfloat16
    )

    dz = lax.dot_general(
        cotangent, w_down, (((1,), (1,)), ((), ())), preferred_element_type=jnp.float32
    )
    da = (dz * b * sig * (1.0 + a * (1.0 - sig))).astype(jnp.bfloat16)
    db = (dz * act).astype(jnp.bfloat16)
    g_down = lax.dot_general(
        z, cotangent, (((0,), (0,)), ((), ())), preferred_element_type=jnp.float32
    )
    g_gate = lax.dot_general(h2, da, (((0,), (0,)), ((), ())), preferred_element_type=jnp.float32)
    g_up = lax.dot_general(h2, db, (((0,), (0,)), ((), ())), preferred_element_type=jnp.float32)
    own_gate, own_up, own_down = scatter_packed(
        [g_gate, g_up, g_down.reshape(n * per, -1)]
    )
    dh2 = lax.dot_general(da, w_gate, (((1,), (1,)), ((), ())), preferred_element_type=jnp.float32)
    dh2 = dh2 + lax.dot_general(
        db, w_up, (((1,), (1,)), ((), ())), preferred_element_type=jnp.float32
    )
    g_gain2 = jnp.sum(dh2 * resid * s2, axis=0)
    dn2 = dh2 * gain2f
    d_resid = (
        cotangent.astype(jnp.float32)
        + s2 * dn2
        - resid * (s2 * s2 * s2) * jnp.mean(dn2 * resid, axis=-1, keepdims=True)
    )
    d_out = d_resid.astype(jnp.bfloat16)
    g_out = lax.dot_general(y, d_out, (((0,), (0,)), ((), ())), preferred_element_type=jnp.float32)
    dy = lax.dot_general(d_out, w_out, (((1,), (1,)), ((), ())), preferred_element_type=jnp.float32)
    d_cgate = dy * conv_out
    d_conv = dy * cgate
    d_ext = jnp.zeros((rows + 2, width), jnp.float32)
    tap_cols = []
    for k in range(CONV):
        term = d_conv * masks[k]
        d_ext = d_ext + jnp.pad(taps[:, k] * term, ((2 - k, k), (0, 0)))
        tap_cols.append(jnp.sum(term * ext_bx[2 - k : 2 - k + rows], axis=0))
    g_conv = jnp.stack(tap_cols, axis=1)
    returned = shifted(d_ext[:2], "fsdp", -1)
    d_bx = d_ext[2:] + jnp.pad(returned, ((rows - 2, 0), (0, 0)))
    d_proj = jnp.concatenate([d_bx * xv, d_cgate, d_bx * bgate], axis=1).astype(jnp.bfloat16)
    g_in = lax.dot_general(h, d_proj, (((0,), (0,)), ((), ())), preferred_element_type=jnp.float32)
    dh = lax.dot_general(d_proj, w_in, (((1,), (1,)), ((), ())), preferred_element_type=jnp.float32)
    g_gain1 = jnp.sum(dh * xf * s1, axis=0)
    dn1 = dh * gain1.astype(jnp.float32)
    input_grad = (
        d_resid + s1 * dn1 - xf * (s1 * s1 * s1) * jnp.mean(dn1 * xf, axis=-1, keepdims=True)
    )
    g_small = jnp.concatenate([g_gain1[:, None], g_gain2[:, None], g_conv], axis=1)
    own_in, own_out, own_small = scatter_packed([g_in, g_out, pad_cols(g_small)])
    return (
        block_out,
        input_grad,
        own_small[:, 0],
        own_in,
        own_small[:, 2 : 2 + CONV],
        own_out,
        own_small[:, 1],
        own_gate,
        own_up,
        own_down.reshape(down_rows, width),
    )


def solution(mesh):
    return jax.shard_map(
        per_device,
        mesh=mesh,
        in_specs=(
            P("fsdp", None),
            P("fsdp"),
            P("fsdp", None),
            P("fsdp", None),
            P("fsdp", None),
            P("fsdp"),
            P("fsdp", None),
            P("fsdp", None),
            P("fsdp", None),
            P("fsdp"),
            P("fsdp", None),
        ),
        out_specs=(
            P("fsdp", None),
            P("fsdp", None),
            P("fsdp"),
            P("fsdp", None),
            P("fsdp", None),
            P("fsdp", None),
            P("fsdp"),
            P("fsdp", None),
            P("fsdp", None),
            P("fsdp", None),
        ),
        check_vma=False,
    )
```

```python
import jax
import jax.numpy as jnp
from jax import lax
from jax.sharding import PartitionSpec as P

CONV = 3
EPS = 1e-05
LANE = 256


def shifted(value, axis, by):
    size = lax.axis_size(axis)
    pairs = [(i, i + by) for i in range(size) if 0 <= i + by < size]
    return lax.ppermute(value, axis, pairs)


def rms_scale(values):
    return lax.rsqrt(jnp.mean(values * values, axis=-1, keepdims=True) + EPS)


def pad_cols(x):
    extra = (-x.shape[1]) % LANE
    return jnp.pad(x, ((0, 0), (0, extra))) if extra else x


def gather_packed(pieces):
    widths = [p.shape[1] for p in pieces]
    packed = jnp.concatenate(pieces, axis=1)
    full = lax.all_gather(packed, "fsdp", axis=0, tiled=True)
    out, at = [], 0
    for w in widths:
        out.append(full[:, at : at + w])
        at += w
    return out


def scatter_packed(pieces, exchange=True):
    widths = [p.shape[1] for p in pieces]
    packed = jnp.concatenate(pieces, axis=1)
    if exchange:
        n = lax.axis_size("fsdp")
        blocks = lax.all_to_all(
            packed.astype(jnp.bfloat16), "fsdp", 0, 0, tiled=True
        )
        blocks = blocks.reshape(n, blocks.shape[0] // n, blocks.shape[1])
        mine = jnp.sum(blocks.astype(jnp.float32), axis=0)
    else:
        mine = lax.psum_scatter(packed, "fsdp", scatter_dimension=0, tiled=True)
    mine = lax.optimization_barrier(mine)
    out, at = [], 0
    for w in widths:
        out.append(mine[:, at : at + w])
        at += w
    return out


def per_device(
    hidden_in,
    norm1_gain,
    in_weight,
    conv_weight,
    out_weight,
    norm2_gain,
    gate_weight,
    up_weight,
    down_weight,
    segment_ids,
    cotangent,
):
    rows = hidden_in.shape[0]
    width = hidden_in.shape[1]
    per = in_weight.shape[0]
    n = lax.axis_size("fsdp")
    down_rows = down_weight.shape[0]
    small = jnp.concatenate(
        [norm1_gain[:, None], norm2_gain[:, None], conv_weight], axis=1
    )
    n_small = small.shape[1]
    w_in, w_out, small_full = gather_packed([in_weight, out_weight, pad_cols(small)])
    w_gate, w_up, w_down_packed = gather_packed(
        [gate_weight, up_weight, down_weight.reshape(per, -1)]
    )
    w_down = w_down_packed.reshape(n * down_rows, width)
    gain1 = small_full[:, 0]
    gain2 = small_full[:, 1]
    w_conv = small_full[:, 2 : 2 + CONV]

    xf = hidden_in.astype(jnp.float32)
    s1 = rms_scale(xf)
    h = (xf * s1 * gain1.astype(jnp.float32)).astype(jnp.bfloat16)
    proj = jnp.dot(h, w_in, preferred_element_type=jnp.float32)
    bgate = proj[:, :width]
    cgate = proj[:, width : 2 * width]
    xv = proj[:, 2 * width :]
    bx = (bgate * xv).astype(jnp.bfloat16)
    prev_rows, prev_ids = shifted(
        (bx[rows - 2 :], segment_ids[rows - 2 :].astype(jnp.bfloat16)), "fsdp", 1
    )
    ext_bx = jnp.concatenate([prev_rows, bx], axis=0).astype(jnp.float32)
    ext_ids = jnp.concatenate([prev_ids.astype(jnp.int32), segment_ids], axis=0)
    taps = w_conv.astype(jnp.float32)
    masks = [
        (ext_ids[2 - k : 2 - k + rows] == segment_ids).astype(jnp.float32)[:, None]
        for k in range(CONV)
    ]
    conv_out = jnp.zeros((rows, width), jnp.float32)
    for k in range(CONV):
        conv_out = conv_out + taps[:, k] * masks[k] * ext_bx[2 - k : 2 - k + rows]
    y = (cgate * conv_out).astype(jnp.bfloat16)
    resid = xf + jnp.dot(y, w_out, preferred_element_type=jnp.float32)
    s2 = rms_scale(resid)
    gain2f = gain2.astype(jnp.float32)
    h2 = (resid * s2 * gain2f).astype(jnp.bfloat16)
    a = jnp.dot(h2, w_gate, preferred_element_type=jnp.float32)
    b = jnp.dot(h2, w_up, preferred_element_type=jnp.float32)
    sig = jax.nn.sigmoid(a)
    act = a * sig
    z = (act * b).astype(jnp.bfloat16)
    block_out = (resid + jnp.dot(z, w_down, preferred_element_type=jnp.float32)).astype(
        jnp.bfloat16
    )

    dz = lax.dot_general(
        cotangent, w_down, (((1,), (1,)), ((), ())), preferred_element_type=jnp.float32
    )
    da = (dz * b * sig * (1.0 + a * (1.0 - sig))).astype(jnp.bfloat16)
    db = (dz * act).astype(jnp.bfloat16)
    g_down = lax.dot_general(
        z, cotangent, (((0,), (0,)), ((), ())), preferred_element_type=jnp.float32
    )
    g_gate = lax.dot_general(h2, da, (((0,), (0,)), ((), ())), preferred_element_type=jnp.float32)
    g_up = lax.dot_general(h2, db, (((0,), (0,)), ((), ())), preferred_element_type=jnp.float32)
    own_gate, own_up, own_down = scatter_packed(
        [g_gate, g_up, g_down.reshape(n * per, -1)]
    )
    dh2 = lax.dot_general(da, w_gate, (((1,), (1,)), ((), ())), preferred_element_type=jnp.float32)
    dh2 = dh2 + lax.dot_general(
        db, w_up, (((1,), (1,)), ((), ())), preferred_element_type=jnp.float32
    )
    g_gain2 = jnp.sum(dh2 * resid * s2, axis=0)
    dn2 = dh2 * gain2f
    d_resid = (
        cotangent.astype(jnp.float32)
        + s2 * dn2
        - resid * (s2 * s2 * s2) * jnp.mean(dn2 * resid, axis=-1, keepdims=True)
    )
    d_out = d_resid.astype(jnp.bfloat16)
    g_out = lax.dot_general(y, d_out, (((0,), (0,)), ((), ())), preferred_element_type=jnp.float32)
    dy = lax.dot_general(d_out, w_out, (((1,), (1,)), ((), ())), preferred_element_type=jnp.float32)
    d_cgate = dy * conv_out
    d_conv = dy * cgate
    d_ext = jnp.zeros((rows + 2, width), jnp.float32)
    tap_cols = []
    for k in range(CONV):
        term = d_conv * masks[k]
        d_ext = d_ext + jnp.pad(taps[:, k] * term, ((2 - k, k), (0, 0)))
        tap_cols.append(jnp.sum(term * ext_bx[2 - k : 2 - k + rows], axis=0))
    g_conv = jnp.stack(tap_cols, axis=1)
    returned = shifted(d_ext[:2], "fsdp", -1)
    d_bx = d_ext[2:] + jnp.pad(returned, ((rows - 2, 0), (0, 0)))
    d_proj = jnp.concatenate([d_bx * xv, d_cgate, d_bx * bgate], axis=1).astype(jnp.bfloat16)
    g_in = lax.dot_general(h, d_proj, (((0,), (0,)), ((), ())), preferred_element_type=jnp.float32)
    dh = lax.dot_general(d_proj, w_in, (((1,), (1,)), ((), ())), preferred_element_type=jnp.float32)
    g_gain1 = jnp.sum(dh * xf * s1, axis=0)
    dn1 = dh * gain1.astype(jnp.float32)
    input_grad = (
        d_resid + s1 * dn1 - xf * (s1 * s1 * s1) * jnp.mean(dn1 * xf, axis=-1, keepdims=True)
    )
    g_small = jnp.concatenate([g_gain1[:, None], g_gain2[:, None], g_conv], axis=1)
    own_in, own_out = scatter_packed([g_in, g_out])
    (own_small,) = scatter_packed([pad_cols(g_small)], exchange=False)
    return (
        block_out,
        input_grad,
        own_small[:, 0],
        own_in,
        own_small[:, 2 : 2 + CONV],
        own_out,
        own_small[:, 1],
        own_gate,
        own_up,
        own_down.reshape(down_rows, width),
    )


def solution(mesh):
    return jax.shard_map(
        per_device,
        mesh=mesh,
        in_specs=(
            P("fsdp", None),
            P("fsdp"),
            P("fsdp", None),
            P("fsdp", None),
            P("fsdp", None),
            P("fsdp"),
            P("fsdp", None),
            P("fsdp", None),
            P("fsdp", None),
            P("fsdp"),
            P("fsdp", None),
        ),
        out_specs=(
            P("fsdp", None),
            P("fsdp", None),
            P("fsdp"),
            P("fsdp", None),
            P("fsdp", None),
            P("fsdp", None),
            P("fsdp"),
            P("fsdp", None),
            P("fsdp", None),
            P("fsdp", None),
        ),
        check_vma=False,
    )
```

```python
import jax
import jax.numpy as jnp
from jax import lax
from jax.sharding import PartitionSpec as P

CONV = 3
EPS = 1e-05
LANE = 256


def shifted(value, axis, by):
    size = lax.axis_size(axis)
    pairs = [(i, i + by) for i in range(size) if 0 <= i + by < size]
    return lax.ppermute(value, axis, pairs)


def rms_scale(values):
    return lax.rsqrt(jnp.mean(values * values, axis=-1, keepdims=True) + EPS)


def pad_cols(x):
    extra = (-x.shape[1]) % LANE
    return jnp.pad(x, ((0, 0), (0, extra))) if extra else x


def gather_packed(pieces):
    widths = [p.shape[1] for p in pieces]
    packed = jnp.concatenate(pieces, axis=1)
    full = lax.all_gather(packed, "fsdp", axis=0, tiled=True)
    out, at = [], 0
    for w in widths:
        out.append(full[:, at : at + w])
        at += w
    return out


def scatter_packed(pieces, dtype=jnp.bfloat16):
    widths = [p.shape[1] for p in pieces]
    packed = jnp.concatenate(pieces, axis=1)
    n = lax.axis_size("fsdp")
    blocks = lax.all_to_all(packed.astype(dtype), "fsdp", 0, 0, tiled=True)
    blocks = blocks.reshape(n, blocks.shape[0] // n, blocks.shape[1])
    mine = lax.optimization_barrier(jnp.sum(blocks.astype(jnp.float32), axis=0))
    out, at = [], 0
    for w in widths:
        out.append(mine[:, at : at + w])
        at += w
    return out


def per_device(
    hidden_in,
    norm1_gain,
    in_weight,
    conv_weight,
    out_weight,
    norm2_gain,
    gate_weight,
    up_weight,
    down_weight,
    segment_ids,
    cotangent,
):
    rows = hidden_in.shape[0]
    width = hidden_in.shape[1]
    per = in_weight.shape[0]
    n = lax.axis_size("fsdp")
    down_rows = down_weight.shape[0]
    small = jnp.concatenate(
        [norm1_gain[:, None], norm2_gain[:, None], conv_weight], axis=1
    )
    n_small = small.shape[1]
    w_in, w_out, small_full = gather_packed([in_weight, out_weight, pad_cols(small)])
    w_gate, w_up, w_down_packed = gather_packed(
        [gate_weight, up_weight, down_weight.reshape(per, -1)]
    )
    w_down = w_down_packed.reshape(n * down_rows, width)
    gain1 = small_full[:, 0]
    gain2 = small_full[:, 1]
    w_conv = small_full[:, 2 : 2 + CONV]

    xf = hidden_in.astype(jnp.float32)
    s1 = rms_scale(xf)
    h = (xf * s1 * gain1.astype(jnp.float32)).astype(jnp.bfloat16)
    proj = jnp.dot(h, w_in, preferred_element_type=jnp.float32)
    bgate = proj[:, :width]
    cgate = proj[:, width : 2 * width]
    xv = proj[:, 2 * width :]
    bx = (bgate * xv).astype(jnp.bfloat16)
    prev_rows, prev_ids = shifted(
        (bx[rows - 2 :], segment_ids[rows - 2 :].astype(jnp.bfloat16)), "fsdp", 1
    )
    ext_bx = jnp.concatenate([prev_rows, bx], axis=0).astype(jnp.float32)
    ext_ids = jnp.concatenate([prev_ids.astype(jnp.int32), segment_ids], axis=0)
    taps = w_conv.astype(jnp.float32)
    masks = [
        (ext_ids[2 - k : 2 - k + rows] == segment_ids).astype(jnp.float32)[:, None]
        for k in range(CONV)
    ]
    conv_out = jnp.zeros((rows, width), jnp.float32)
    for k in range(CONV):
        conv_out = conv_out + taps[:, k] * masks[k] * ext_bx[2 - k : 2 - k + rows]
    y = (cgate * conv_out).astype(jnp.bfloat16)
    resid = xf + jnp.dot(y, w_out, preferred_element_type=jnp.float32)
    s2 = rms_scale(resid)
    gain2f = gain2.astype(jnp.float32)
    h2 = (resid * s2 * gain2f).astype(jnp.bfloat16)
    a = jnp.dot(h2, w_gate, preferred_element_type=jnp.float32)
    b = jnp.dot(h2, w_up, preferred_element_type=jnp.float32)
    sig = jax.nn.sigmoid(a)
    act = a * sig
    z = (act * b).astype(jnp.bfloat16)
    block_out = (resid + jnp.dot(z, w_down, preferred_element_type=jnp.float32)).astype(
        jnp.bfloat16
    )

    dz = lax.dot_general(
        cotangent, w_down, (((1,), (1,)), ((), ())), preferred_element_type=jnp.float32
    )
    da = (dz * b * sig * (1.0 + a * (1.0 - sig))).astype(jnp.bfloat16)
    db = (dz * act).astype(jnp.bfloat16)
    g_down = lax.dot_general(
        z, cotangent, (((0,), (0,)), ((), ())), preferred_element_type=jnp.float32
    )
    g_gate = lax.dot_general(h2, da, (((0,), (0,)), ((), ())), preferred_element_type=jnp.float32)
    g_up = lax.dot_general(h2, db, (((0,), (0,)), ((), ())), preferred_element_type=jnp.float32)
    own_gate, own_up, own_down = scatter_packed(
        [g_gate, g_up, g_down.reshape(n * per, -1)]
    )
    dh2 = lax.dot_general(da, w_gate, (((1,), (1,)), ((), ())), preferred_element_type=jnp.float32)
    dh2 = dh2 + lax.dot_general(
        db, w_up, (((1,), (1,)), ((), ())), preferred_element_type=jnp.float32
    )
    g_gain2 = jnp.sum(dh2 * resid * s2, axis=0)
    dn2 = dh2 * gain2f
    d_resid = (
        cotangent.astype(jnp.float32)
        + s2 * dn2
        - resid * (s2 * s2 * s2) * jnp.mean(dn2 * resid, axis=-1, keepdims=True)
    )
    d_out = d_resid.astype(jnp.bfloat16)
    g_out = lax.dot_general(y, d_out, (((0,), (0,)), ((), ())), preferred_element_type=jnp.float32)
    dy = lax.dot_general(d_out, w_out, (((1,), (1,)), ((), ())), preferred_element_type=jnp.float32)
    d_cgate = dy * conv_out
    d_conv = dy * cgate
    d_ext = jnp.zeros((rows + 2, width), jnp.float32)
    tap_cols = []
    for k in range(CONV):
        term = d_conv * masks[k]
        d_ext = d_ext + jnp.pad(taps[:, k] * term, ((2 - k, k), (0, 0)))
        tap_cols.append(jnp.sum(term * ext_bx[2 - k : 2 - k + rows], axis=0))
    g_conv = jnp.stack(tap_cols, axis=1)
    returned = shifted(d_ext[:2], "fsdp", -1)
    d_bx = d_ext[2:] + jnp.pad(returned, ((rows - 2, 0), (0, 0)))
    d_proj = jnp.concatenate([d_bx * xv, d_cgate, d_bx * bgate], axis=1).astype(jnp.bfloat16)
    g_in = lax.dot_general(h, d_proj, (((0,), (0,)), ((), ())), preferred_element_type=jnp.float32)
    dh = lax.dot_general(d_proj, w_in, (((1,), (1,)), ((), ())), preferred_element_type=jnp.float32)
    g_gain1 = jnp.sum(dh * xf * s1, axis=0)
    dn1 = dh * gain1.astype(jnp.float32)
    input_grad = (
        d_resid + s1 * dn1 - xf * (s1 * s1 * s1) * jnp.mean(dn1 * xf, axis=-1, keepdims=True)
    )
    g_small = jnp.concatenate([g_gain1[:, None], g_gain2[:, None], g_conv], axis=1)
    own_in, own_out = scatter_packed([g_in, g_out])
    (own_small,) = scatter_packed([pad_cols(g_small)], dtype=jnp.float32)
    return (
        block_out,
        input_grad,
        own_small[:, 0],
        own_in,
        own_small[:, 2 : 2 + CONV],
        own_out,
        own_small[:, 1],
        own_gate,
        own_up,
        own_down.reshape(down_rows, width),
    )


def solution(mesh):
    return jax.shard_map(
        per_device,
        mesh=mesh,
        in_specs=(
            P("fsdp", None),
            P("fsdp"),
            P("fsdp", None),
            P("fsdp", None),
            P("fsdp", None),
            P("fsdp"),
            P("fsdp", None),
            P("fsdp", None),
            P("fsdp", None),
            P("fsdp"),
            P("fsdp", None),
        ),
        out_specs=(
            P("fsdp", None),
            P("fsdp", None),
            P("fsdp"),
            P("fsdp", None),
            P("fsdp", None),
            P("fsdp", None),
            P("fsdp"),
            P("fsdp", None),
            P("fsdp", None),
            P("fsdp", None),
        ),
        check_vma=False,
    )
```

```python
import jax
import jax.numpy as jnp
from jax import lax
from jax.sharding import PartitionSpec as P

CONV = 3
EPS = 1e-05
LANE = 256


def shifted(value, axis, by):
    size = lax.axis_size(axis)
    pairs = [(i, i + by) for i in range(size) if 0 <= i + by < size]
    return lax.ppermute(value, axis, pairs)


def rms_scale(values):
    return lax.rsqrt(jnp.mean(values * values, axis=-1, keepdims=True) + EPS)


def pad_cols(x):
    extra = (-x.shape[1]) % LANE
    return jnp.pad(x, ((0, 0), (0, extra))) if extra else x


def gather_packed(pieces):
    widths = [p.shape[1] for p in pieces]
    packed = jnp.concatenate(pieces, axis=1)
    full = lax.all_gather(packed, AXES, axis=0, tiled=True)
    out, at = [], 0
    for w in widths:
        out.append(full[:, at : at + w])
        at += w
    return out


AXES = ("y", "z", "x", "core")
FSDP = AXES


def exchange_packed(pieces, dtype=jnp.float32):
    widths = [p.shape[1] for p in pieces]
    packed = jnp.concatenate(pieces, axis=1)
    n = lax.axis_size(AXES)
    blocks = lax.all_to_all(packed.astype(dtype), AXES, 0, 0, tiled=True)
    blocks = blocks.reshape(n, blocks.shape[0] // n, blocks.shape[1])
    mine = lax.optimization_barrier(jnp.sum(blocks.astype(jnp.float32), axis=0))
    out, at = [], 0
    for w in widths:
        out.append(mine[:, at : at + w])
        at += w
    return out


def scatter_packed(pieces, dtype=jnp.bfloat16):
    widths = [p.shape[1] for p in pieces]
    packed = jnp.concatenate(pieces, axis=1).astype(dtype)
    sizes = [lax.axis_size(a) for a in AXES]
    per = packed.shape[0] // (sizes[0] * sizes[1] * sizes[2] * sizes[3])
    blocks = packed.reshape(sizes + [per, packed.shape[1]])
    blocks = blocks.transpose(3, 2, 1, 0, 4, 5).reshape(packed.shape)
    for axis in reversed(AXES):
        blocks = lax.psum_scatter(blocks, axis, scatter_dimension=0, tiled=True)
    mine = lax.optimization_barrier(blocks).astype(jnp.float32)
    out, at = [], 0
    for w in widths:
        out.append(mine[:, at : at + w])
        at += w
    return out


def per_device(
    hidden_in,
    norm1_gain,
    in_weight,
    conv_weight,
    out_weight,
    norm2_gain,
    gate_weight,
    up_weight,
    down_weight,
    segment_ids,
    cotangent,
):
    rows = hidden_in.shape[0]
    width = hidden_in.shape[1]
    per = in_weight.shape[0]
    n = lax.axis_size(AXES)
    down_rows = down_weight.shape[0]
    small = jnp.concatenate(
        [norm1_gain[:, None], norm2_gain[:, None], conv_weight], axis=1
    )
    n_small = small.shape[1]
    w_in, w_out, small_full = gather_packed([in_weight, out_weight, pad_cols(small)])
    w_gate, w_up, w_down_packed = gather_packed(
        [gate_weight, up_weight, down_weight.reshape(per, -1)]
    )
    w_down = w_down_packed.reshape(n * down_rows, width)
    gain1 = small_full[:, 0]
    gain2 = small_full[:, 1]
    w_conv = small_full[:, 2 : 2 + CONV]

    xf = hidden_in.astype(jnp.float32)
    s1 = rms_scale(xf)
    h = (xf * s1 * gain1.astype(jnp.float32)).astype(jnp.bfloat16)
    proj = jnp.dot(h, w_in, preferred_element_type=jnp.float32)
    bgate = proj[:, :width]
    cgate = proj[:, width : 2 * width]
    xv = proj[:, 2 * width :]
    bx = (bgate * xv).astype(jnp.bfloat16)
    prev_rows, prev_ids = shifted(
        (bx[rows - 2 :], segment_ids[rows - 2 :].astype(jnp.bfloat16)), AXES, 1
    )
    ext_bx = jnp.concatenate([prev_rows, bx], axis=0).astype(jnp.float32)
    ext_ids = jnp.concatenate([prev_ids.astype(jnp.int32), segment_ids], axis=0)
    taps = w_conv.astype(jnp.float32)
    masks = [
        (ext_ids[2 - k : 2 - k + rows] == segment_ids).astype(jnp.float32)[:, None]
        for k in range(CONV)
    ]
    conv_out = jnp.zeros((rows, width), jnp.float32)
    for k in range(CONV):
        conv_out = conv_out + taps[:, k] * masks[k] * ext_bx[2 - k : 2 - k + rows]
    y = (cgate * conv_out).astype(jnp.bfloat16)
    resid = xf + jnp.dot(y, w_out, preferred_element_type=jnp.float32)
    s2 = rms_scale(resid)
    gain2f = gain2.astype(jnp.float32)
    h2 = (resid * s2 * gain2f).astype(jnp.bfloat16)
    a = jnp.dot(h2, w_gate, preferred_element_type=jnp.float32)
    b = jnp.dot(h2, w_up, preferred_element_type=jnp.float32)
    sig = jax.nn.sigmoid(a)
    act = a * sig
    z = (act * b).astype(jnp.bfloat16)
    block_out = (resid + jnp.dot(z, w_down, preferred_element_type=jnp.float32)).astype(
        jnp.bfloat16
    )

    dz = lax.dot_general(
        cotangent, w_down, (((1,), (1,)), ((), ())), preferred_element_type=jnp.float32
    )
    da = (dz * b * sig * (1.0 + a * (1.0 - sig))).astype(jnp.bfloat16)
    db = (dz * act).astype(jnp.bfloat16)
    g_down = lax.dot_general(
        z, cotangent, (((0,), (0,)), ((), ())), preferred_element_type=jnp.float32
    )
    g_gate = lax.dot_general(h2, da, (((0,), (0,)), ((), ())), preferred_element_type=jnp.float32)
    g_up = lax.dot_general(h2, db, (((0,), (0,)), ((), ())), preferred_element_type=jnp.float32)
    own_gate, own_up, own_down = scatter_packed(
        [g_gate, g_up, g_down.reshape(n * per, -1)]
    )
    dh2 = lax.dot_general(da, w_gate, (((1,), (1,)), ((), ())), preferred_element_type=jnp.float32)
    dh2 = dh2 + lax.dot_general(
        db, w_up, (((1,), (1,)), ((), ())), preferred_element_type=jnp.float32
    )
    g_gain2 = jnp.sum(dh2 * resid * s2, axis=0)
    dn2 = dh2 * gain2f
    d_resid = (
        cotangent.astype(jnp.float32)
        + s2 * dn2
        - resid * (s2 * s2 * s2) * jnp.mean(dn2 * resid, axis=-1, keepdims=True)
    )
    d_out = d_resid.astype(jnp.bfloat16)
    g_out = lax.dot_general(y, d_out, (((0,), (0,)), ((), ())), preferred_element_type=jnp.float32)
    dy = lax.dot_general(d_out, w_out, (((1,), (1,)), ((), ())), preferred_element_type=jnp.float32)
    d_cgate = dy * conv_out
    d_conv = dy * cgate
    d_ext = jnp.zeros((rows + 2, width), jnp.float32)
    tap_cols = []
    for k in range(CONV):
        term = d_conv * masks[k]
        d_ext = d_ext + jnp.pad(taps[:, k] * term, ((2 - k, k), (0, 0)))
        tap_cols.append(jnp.sum(term * ext_bx[2 - k : 2 - k + rows], axis=0))
    g_conv = jnp.stack(tap_cols, axis=1)
    returned = shifted(d_ext[:2], AXES, -1)
    d_bx = d_ext[2:] + jnp.pad(returned, ((rows - 2, 0), (0, 0)))
    d_proj = jnp.concatenate([d_bx * xv, d_cgate, d_bx * bgate], axis=1).astype(jnp.bfloat16)
    g_in = lax.dot_general(h, d_proj, (((0,), (0,)), ((), ())), preferred_element_type=jnp.float32)
    dh = lax.dot_general(d_proj, w_in, (((1,), (1,)), ((), ())), preferred_element_type=jnp.float32)
    g_gain1 = jnp.sum(dh * xf * s1, axis=0)
    dn1 = dh * gain1.astype(jnp.float32)
    input_grad = (
        d_resid + s1 * dn1 - xf * (s1 * s1 * s1) * jnp.mean(dn1 * xf, axis=-1, keepdims=True)
    )
    g_small = jnp.concatenate([g_gain1[:, None], g_gain2[:, None], g_conv], axis=1)
    own_in, own_out = scatter_packed([g_in, g_out])
    (own_small,) = exchange_packed([pad_cols(g_small)])
    return (
        block_out,
        input_grad,
        own_small[:, 0],
        own_in,
        own_small[:, 2 : 2 + CONV],
        own_out,
        own_small[:, 1],
        own_gate,
        own_up,
        own_down.reshape(down_rows, width),
    )


def solution(mesh):
    torus = jax.sharding.Mesh(mesh.devices.reshape(4, 4, 4, 2), AXES)
    return jax.shard_map(
        per_device,
        mesh=torus,
        in_specs=(
            P(FSDP, None),
            P(FSDP),
            P(FSDP, None),
            P(FSDP, None),
            P(FSDP, None),
            P(FSDP),
            P(FSDP, None),
            P(FSDP, None),
            P(FSDP, None),
            P(FSDP),
            P(FSDP, None),
        ),
        out_specs=(
            P(FSDP, None),
            P(FSDP, None),
            P(FSDP),
            P(FSDP, None),
            P(FSDP, None),
            P(FSDP, None),
            P(FSDP),
            P(FSDP, None),
            P(FSDP, None),
            P(FSDP, None),
        ),
        check_vma=False,
    )
```

```python
import jax
import jax.numpy as jnp
from jax import lax
from jax.sharding import PartitionSpec as P

CONV = 3
EPS = 1e-05
LANE = 256


def shifted(value, axis, by):
    size = lax.axis_size(axis)
    pairs = [(i, i + by) for i in range(size) if 0 <= i + by < size]
    return lax.ppermute(value, axis, pairs)


def rms_scale(values):
    return lax.rsqrt(jnp.mean(values * values, axis=-1, keepdims=True) + EPS)


def pad_cols(x):
    extra = (-x.shape[1]) % LANE
    return jnp.pad(x, ((0, 0), (0, extra))) if extra else x


def gather_packed(pieces):
    widths = [p.shape[1] for p in pieces]
    packed = jnp.concatenate(pieces, axis=1)
    full = lax.all_gather(packed, AXES, axis=0, tiled=True)
    out, at = [], 0
    for w in widths:
        out.append(full[:, at : at + w])
        at += w
    return out


AXES = ("y", "z", "x", "core")
FSDP = AXES


def exchange_packed(pieces, dtype=jnp.float32):
    widths = [p.shape[1] for p in pieces]
    packed = jnp.concatenate(pieces, axis=1)
    n = lax.axis_size(AXES)
    blocks = lax.all_to_all(packed.astype(dtype), AXES, 0, 0, tiled=True)
    blocks = blocks.reshape(n, blocks.shape[0] // n, blocks.shape[1])
    mine = lax.optimization_barrier(jnp.sum(blocks.astype(jnp.float32), axis=0))
    out, at = [], 0
    for w in widths:
        out.append(mine[:, at : at + w])
        at += w
    return out


def scatter_packed(pieces, order=("core", "x", "z", "y"), direct=False):
    widths = [p.shape[1] for p in pieces]
    packed = jnp.concatenate(pieces, axis=1).astype(jnp.bfloat16)
    sizes = [lax.axis_size(a) for a in AXES]
    count = sizes[0] * sizes[1] * sizes[2] * sizes[3]
    per = packed.shape[0] // count
    blocks = packed.reshape(sizes + [per, packed.shape[1]])
    blocks = blocks.transpose([AXES.index(a) for a in order] + [4, 5])
    blocks = blocks.reshape(packed.shape)
    for axis in order:
        if direct:
            size = lax.axis_size(axis)
            got = lax.all_to_all(blocks, axis, 0, 0, tiled=True)
            got = got.reshape(size, got.shape[0] // size, got.shape[1])
            blocks = jnp.sum(got.astype(jnp.float32), axis=0).astype(jnp.bfloat16)
        else:
            blocks = lax.psum_scatter(blocks, axis, scatter_dimension=0, tiled=True)
    mine = lax.optimization_barrier(blocks).astype(jnp.float32)
    out, at = [], 0
    for w in widths:
        out.append(mine[:, at : at + w])
        at += w
    return out


def per_device(
    hidden_in,
    norm1_gain,
    in_weight,
    conv_weight,
    out_weight,
    norm2_gain,
    gate_weight,
    up_weight,
    down_weight,
    segment_ids,
    cotangent,
):
    rows = hidden_in.shape[0]
    width = hidden_in.shape[1]
    per = in_weight.shape[0]
    n = lax.axis_size(AXES)
    down_rows = down_weight.shape[0]
    small = jnp.concatenate(
        [norm1_gain[:, None], norm2_gain[:, None], conv_weight], axis=1
    )
    n_small = small.shape[1]
    w_in, w_out, small_full = gather_packed([in_weight, out_weight, pad_cols(small)])
    w_gate, w_up, w_down_packed = gather_packed(
        [gate_weight, up_weight, down_weight.reshape(per, -1)]
    )
    w_down = w_down_packed.reshape(n * down_rows, width)
    gain1 = small_full[:, 0]
    gain2 = small_full[:, 1]
    w_conv = small_full[:, 2 : 2 + CONV]

    xf = hidden_in.astype(jnp.float32)
    s1 = rms_scale(xf)
    h = (xf * s1 * gain1.astype(jnp.float32)).astype(jnp.bfloat16)
    proj = jnp.dot(h, w_in, preferred_element_type=jnp.float32)
    bgate = proj[:, :width]
    cgate = proj[:, width : 2 * width]
    xv = proj[:, 2 * width :]
    bx = (bgate * xv).astype(jnp.bfloat16)
    prev_rows, prev_ids = shifted(
        (bx[rows - 2 :], segment_ids[rows - 2 :].astype(jnp.bfloat16)), AXES, 1
    )
    ext_bx = jnp.concatenate([prev_rows, bx], axis=0).astype(jnp.float32)
    ext_ids = jnp.concatenate([prev_ids.astype(jnp.int32), segment_ids], axis=0)
    taps = w_conv.astype(jnp.float32)
    masks = [
        (ext_ids[2 - k : 2 - k + rows] == segment_ids).astype(jnp.float32)[:, None]
        for k in range(CONV)
    ]
    conv_out = jnp.zeros((rows, width), jnp.float32)
    for k in range(CONV):
        conv_out = conv_out + taps[:, k] * masks[k] * ext_bx[2 - k : 2 - k + rows]
    y = (cgate * conv_out).astype(jnp.bfloat16)
    resid = xf + jnp.dot(y, w_out, preferred_element_type=jnp.float32)
    s2 = rms_scale(resid)
    gain2f = gain2.astype(jnp.float32)
    h2 = (resid * s2 * gain2f).astype(jnp.bfloat16)
    a = jnp.dot(h2, w_gate, preferred_element_type=jnp.float32)
    b = jnp.dot(h2, w_up, preferred_element_type=jnp.float32)
    sig = jax.nn.sigmoid(a)
    act = a * sig
    z = (act * b).astype(jnp.bfloat16)
    block_out = (resid + jnp.dot(z, w_down, preferred_element_type=jnp.float32)).astype(
        jnp.bfloat16
    )

    dz = lax.dot_general(
        cotangent, w_down, (((1,), (1,)), ((), ())), preferred_element_type=jnp.float32
    )
    da = (dz * b * sig * (1.0 + a * (1.0 - sig))).astype(jnp.bfloat16)
    db = (dz * act).astype(jnp.bfloat16)
    g_down = lax.dot_general(
        z, cotangent, (((0,), (0,)), ((), ())), preferred_element_type=jnp.float32
    )
    g_gate = lax.dot_general(h2, da, (((0,), (0,)), ((), ())), preferred_element_type=jnp.float32)
    g_up = lax.dot_general(h2, db, (((0,), (0,)), ((), ())), preferred_element_type=jnp.float32)
    own_gate, own_up = scatter_packed([g_gate, g_up])
    (own_down,) = scatter_packed(
        [g_down.reshape(n * per, -1)], order=("core", "z", "y", "x"), direct=True
    )
    dh2 = lax.dot_general(da, w_gate, (((1,), (1,)), ((), ())), preferred_element_type=jnp.float32)
    dh2 = dh2 + lax.dot_general(
        db, w_up, (((1,), (1,)), ((), ())), preferred_element_type=jnp.float32
    )
    g_gain2 = jnp.sum(dh2 * resid * s2, axis=0)
    dn2 = dh2 * gain2f
    d_resid = (
        cotangent.astype(jnp.float32)
        + s2 * dn2
        - resid * (s2 * s2 * s2) * jnp.mean(dn2 * resid, axis=-1, keepdims=True)
    )
    d_out = d_resid.astype(jnp.bfloat16)
    g_out = lax.dot_general(y, d_out, (((0,), (0,)), ((), ())), preferred_element_type=jnp.float32)
    dy = lax.dot_general(d_out, w_out, (((1,), (1,)), ((), ())), preferred_element_type=jnp.float32)
    d_cgate = dy * conv_out
    d_conv = dy * cgate
    d_ext = jnp.zeros((rows + 2, width), jnp.float32)
    tap_cols = []
    for k in range(CONV):
        term = d_conv * masks[k]
        d_ext = d_ext + jnp.pad(taps[:, k] * term, ((2 - k, k), (0, 0)))
        tap_cols.append(jnp.sum(term * ext_bx[2 - k : 2 - k + rows], axis=0))
    g_conv = jnp.stack(tap_cols, axis=1)
    returned = shifted(d_ext[:2], AXES, -1)
    d_bx = d_ext[2:] + jnp.pad(returned, ((rows - 2, 0), (0, 0)))
    d_proj = jnp.concatenate([d_bx * xv, d_cgate, d_bx * bgate], axis=1).astype(jnp.bfloat16)
    g_in = lax.dot_general(h, d_proj, (((0,), (0,)), ((), ())), preferred_element_type=jnp.float32)
    dh = lax.dot_general(d_proj, w_in, (((1,), (1,)), ((), ())), preferred_element_type=jnp.float32)
    g_gain1 = jnp.sum(dh * xf * s1, axis=0)
    dn1 = dh * gain1.astype(jnp.float32)
    input_grad = (
        d_resid + s1 * dn1 - xf * (s1 * s1 * s1) * jnp.mean(dn1 * xf, axis=-1, keepdims=True)
    )
    g_small = jnp.concatenate([g_gain1[:, None], g_gain2[:, None], g_conv], axis=1)
    own_in, own_out = scatter_packed(
        [g_in, g_out], order=("core", "y", "x", "z"), direct=True
    )
    (own_small,) = exchange_packed([pad_cols(g_small)])
    return (
        block_out,
        input_grad,
        own_small[:, 0],
        own_in,
        own_small[:, 2 : 2 + CONV],
        own_out,
        own_small[:, 1],
        own_gate,
        own_up,
        own_down.reshape(down_rows, width),
    )


def solution(mesh):
    torus = jax.sharding.Mesh(mesh.devices.reshape(4, 4, 4, 2), AXES)
    return jax.shard_map(
        per_device,
        mesh=torus,
        in_specs=(
            P(FSDP, None),
            P(FSDP),
            P(FSDP, None),
            P(FSDP, None),
            P(FSDP, None),
            P(FSDP),
            P(FSDP, None),
            P(FSDP, None),
            P(FSDP, None),
            P(FSDP),
            P(FSDP, None),
        ),
        out_specs=(
            P(FSDP, None),
            P(FSDP, None),
            P(FSDP),
            P(FSDP, None),
            P(FSDP, None),
            P(FSDP, None),
            P(FSDP),
            P(FSDP, None),
            P(FSDP, None),
            P(FSDP, None),
        ),
        check_vma=False,
    )
```

```python
import jax
import jax.numpy as jnp
from jax import lax
from jax.sharding import PartitionSpec as P

CONV = 3
EPS = 1e-05
LANE = 256


def shifted(value, axis, by):
    size = lax.axis_size(axis)
    pairs = [(i, i + by) for i in range(size) if 0 <= i + by < size]
    return lax.ppermute(value, axis, pairs)


def rms_scale(values):
    return lax.rsqrt(jnp.mean(values * values, axis=-1, keepdims=True) + EPS)


def pad_cols(x):
    extra = (-x.shape[1]) % LANE
    return jnp.pad(x, ((0, 0), (0, extra))) if extra else x


def gather_packed(pieces):
    widths = [p.shape[1] for p in pieces]
    packed = jnp.concatenate(pieces, axis=1)
    full = lax.all_gather(packed, AXES, axis=0, tiled=True)
    out, at = [], 0
    for w in widths:
        out.append(full[:, at : at + w])
        at += w
    return out


AXES = ("y", "z", "x", "core")
FSDP = AXES


def exchange_packed(pieces, dtype=jnp.float32):
    widths = [p.shape[1] for p in pieces]
    packed = jnp.concatenate(pieces, axis=1)
    n = lax.axis_size(AXES)
    blocks = lax.all_to_all(packed.astype(dtype), AXES, 0, 0, tiled=True)
    blocks = blocks.reshape(n, blocks.shape[0] // n, blocks.shape[1])
    mine = lax.optimization_barrier(jnp.sum(blocks.astype(jnp.float32), axis=0))
    out, at = [], 0
    for w in widths:
        out.append(mine[:, at : at + w])
        at += w
    return out


def scatter_packed(pieces, order=("core", "x", "z", "y"), direct=False):
    widths = [p.shape[1] for p in pieces]
    packed = jnp.concatenate(pieces, axis=1).astype(jnp.bfloat16)
    sizes = [lax.axis_size(a) for a in AXES]
    count = sizes[0] * sizes[1] * sizes[2] * sizes[3]
    per = packed.shape[0] // count
    blocks = packed.reshape(sizes + [per, packed.shape[1]])
    blocks = blocks.transpose([AXES.index(a) for a in order] + [4, 5])
    blocks = blocks.reshape(packed.shape)
    for axis in order:
        if direct:
            size = lax.axis_size(axis)
            got = lax.all_to_all(blocks, axis, 0, 0, tiled=True)
            got = got.reshape(size, got.shape[0] // size, got.shape[1])
            blocks = jnp.sum(got.astype(jnp.float32), axis=0).astype(jnp.bfloat16)
        else:
            blocks = lax.psum_scatter(blocks, axis, scatter_dimension=0, tiled=True)
    mine = lax.optimization_barrier(blocks).astype(jnp.float32)
    out, at = [], 0
    for w in widths:
        out.append(mine[:, at : at + w])
        at += w
    return out


def per_device(
    hidden_in,
    norm1_gain,
    in_weight,
    conv_weight,
    out_weight,
    norm2_gain,
    gate_weight,
    up_weight,
    down_weight,
    segment_ids,
    cotangent,
):
    rows = hidden_in.shape[0]
    width = hidden_in.shape[1]
    per = in_weight.shape[0]
    n = lax.axis_size(AXES)
    down_rows = down_weight.shape[0]
    small = jnp.concatenate(
        [norm1_gain[:, None], norm2_gain[:, None], conv_weight], axis=1
    )
    n_small = small.shape[1]
    w_in, w_out, small_full, w_gate, w_up, w_down_packed = gather_packed(
        [
            in_weight,
            out_weight,
            pad_cols(small),
            gate_weight,
            up_weight,
            down_weight.reshape(per, -1),
        ]
    )
    w_down = w_down_packed.reshape(n * down_rows, width)
    gain1 = small_full[:, 0]
    gain2 = small_full[:, 1]
    w_conv = small_full[:, 2 : 2 + CONV]

    xf = hidden_in.astype(jnp.float32)
    s1 = rms_scale(xf)
    h = (xf * s1 * gain1.astype(jnp.float32)).astype(jnp.bfloat16)
    proj = jnp.dot(h, w_in, preferred_element_type=jnp.float32)
    bgate = proj[:, :width]
    cgate = proj[:, width : 2 * width]
    xv = proj[:, 2 * width :]
    bx = (bgate * xv).astype(jnp.bfloat16)
    prev_rows, prev_ids = shifted(
        (bx[rows - 2 :], segment_ids[rows - 2 :].astype(jnp.bfloat16)), AXES, 1
    )
    ext_bx = jnp.concatenate([prev_rows, bx], axis=0).astype(jnp.float32)
    ext_ids = jnp.concatenate([prev_ids.astype(jnp.int32), segment_ids], axis=0)
    taps = w_conv.astype(jnp.float32)
    masks = [
        (ext_ids[2 - k : 2 - k + rows] == segment_ids).astype(jnp.float32)[:, None]
        for k in range(CONV)
    ]
    conv_out = jnp.zeros((rows, width), jnp.float32)
    for k in range(CONV):
        conv_out = conv_out + taps[:, k] * masks[k] * ext_bx[2 - k : 2 - k + rows]
    y = (cgate * conv_out).astype(jnp.bfloat16)
    resid = xf + jnp.dot(y, w_out, preferred_element_type=jnp.float32)
    s2 = rms_scale(resid)
    gain2f = gain2.astype(jnp.float32)
    h2 = (resid * s2 * gain2f).astype(jnp.bfloat16)
    a = jnp.dot(h2, w_gate, preferred_element_type=jnp.float32)
    b = jnp.dot(h2, w_up, preferred_element_type=jnp.float32)
    sig = jax.nn.sigmoid(a)
    act = a * sig
    z = (act * b).astype(jnp.bfloat16)
    block_out = (resid + jnp.dot(z, w_down, preferred_element_type=jnp.float32)).astype(
        jnp.bfloat16
    )

    dz = lax.dot_general(
        cotangent, w_down, (((1,), (1,)), ((), ())), preferred_element_type=jnp.float32
    )
    da = (dz * b * sig * (1.0 + a * (1.0 - sig))).astype(jnp.bfloat16)
    db = (dz * act).astype(jnp.bfloat16)
    g_down = lax.dot_general(
        z, cotangent, (((0,), (0,)), ((), ())), preferred_element_type=jnp.float32
    )
    g_gate = lax.dot_general(h2, da, (((0,), (0,)), ((), ())), preferred_element_type=jnp.float32)
    g_up = lax.dot_general(h2, db, (((0,), (0,)), ((), ())), preferred_element_type=jnp.float32)
    own_gate, own_up = scatter_packed([g_gate, g_up])
    (own_down,) = scatter_packed(
        [g_down.reshape(n * per, -1)], order=("core", "z", "y", "x"), direct=True
    )
    dh2 = lax.dot_general(da, w_gate, (((1,), (1,)), ((), ())), preferred_element_type=jnp.float32)
    dh2 = dh2 + lax.dot_general(
        db, w_up, (((1,), (1,)), ((), ())), preferred_element_type=jnp.float32
    )
    g_gain2 = jnp.sum(dh2 * resid * s2, axis=0)
    dn2 = dh2 * gain2f
    d_resid = (
        cotangent.astype(jnp.float32)
        + s2 * dn2
        - resid * (s2 * s2 * s2) * jnp.mean(dn2 * resid, axis=-1, keepdims=True)
    )
    d_out = d_resid.astype(jnp.bfloat16)
    g_out = lax.dot_general(y, d_out, (((0,), (0,)), ((), ())), preferred_element_type=jnp.float32)
    dy = lax.dot_general(d_out, w_out, (((1,), (1,)), ((), ())), preferred_element_type=jnp.float32)
    d_cgate = dy * conv_out
    d_conv = dy * cgate
    d_ext = jnp.zeros((rows + 2, width), jnp.float32)
    tap_cols = []
    for k in range(CONV):
        term = d_conv * masks[k]
        d_ext = d_ext + jnp.pad(taps[:, k] * term, ((2 - k, k), (0, 0)))
        tap_cols.append(jnp.sum(term * ext_bx[2 - k : 2 - k + rows], axis=0))
    g_conv = jnp.stack(tap_cols, axis=1)
    returned = shifted(d_ext[:2], AXES, -1)
    d_bx = d_ext[2:] + jnp.pad(returned, ((rows - 2, 0), (0, 0)))
    d_proj = jnp.concatenate([d_bx * xv, d_cgate, d_bx * bgate], axis=1).astype(jnp.bfloat16)
    g_in = lax.dot_general(h, d_proj, (((0,), (0,)), ((), ())), preferred_element_type=jnp.float32)
    dh = lax.dot_general(d_proj, w_in, (((1,), (1,)), ((), ())), preferred_element_type=jnp.float32)
    g_gain1 = jnp.sum(dh * xf * s1, axis=0)
    dn1 = dh * gain1.astype(jnp.float32)
    input_grad = (
        d_resid + s1 * dn1 - xf * (s1 * s1 * s1) * jnp.mean(dn1 * xf, axis=-1, keepdims=True)
    )
    g_small = jnp.concatenate([g_gain1[:, None], g_gain2[:, None], g_conv], axis=1)
    own_in, own_out = scatter_packed(
        [g_in, g_out], order=("core", "y", "x", "z"), direct=True
    )
    (own_small,) = exchange_packed([pad_cols(g_small)])
    return (
        block_out,
        input_grad,
        own_small[:, 0],
        own_in,
        own_small[:, 2 : 2 + CONV],
        own_out,
        own_small[:, 1],
        own_gate,
        own_up,
        own_down.reshape(down_rows, width),
    )


def solution(mesh):
    torus = jax.sharding.Mesh(mesh.devices.reshape(4, 4, 4, 2), AXES)
    return jax.shard_map(
        per_device,
        mesh=torus,
        in_specs=(
            P(FSDP, None),
            P(FSDP),
            P(FSDP, None),
            P(FSDP, None),
            P(FSDP, None),
            P(FSDP),
            P(FSDP, None),
            P(FSDP, None),
            P(FSDP, None),
            P(FSDP),
            P(FSDP, None),
        ),
        out_specs=(
            P(FSDP, None),
            P(FSDP, None),
            P(FSDP),
            P(FSDP, None),
            P(FSDP, None),
            P(FSDP, None),
            P(FSDP),
            P(FSDP, None),
            P(FSDP, None),
            P(FSDP, None),
        ),
        check_vma=False,
    )
```

```python
import jax
import jax.numpy as jnp
from jax import lax
from jax.sharding import PartitionSpec as P

CONV = 3
EPS = 1e-05
LANE = 256


def shifted(value, axis, by):
    size = lax.axis_size(axis)
    pairs = [(i, i + by) for i in range(size) if 0 <= i + by < size]
    return lax.ppermute(value, axis, pairs)


def rms_scale(values):
    return lax.rsqrt(jnp.mean(values * values, axis=-1, keepdims=True) + EPS)


def pad_cols(x):
    extra = (-x.shape[1]) % LANE
    return jnp.pad(x, ((0, 0), (0, extra))) if extra else x


def gather_packed(pieces):
    widths = [p.shape[1] for p in pieces]
    packed = jnp.concatenate(pieces, axis=1)
    full = lax.all_gather(packed, AXES, axis=0, tiled=True)
    out, at = [], 0
    for w in widths:
        out.append(full[:, at : at + w])
        at += w
    return out


AXES = ("y", "z", "x", "core")
FSDP = AXES


def exchange_packed(pieces, dtype=jnp.float32):
    widths = [p.shape[1] for p in pieces]
    packed = jnp.concatenate(pieces, axis=1)
    n = lax.axis_size(AXES)
    blocks = lax.all_to_all(packed.astype(dtype), AXES, 0, 0, tiled=True)
    blocks = blocks.reshape(n, blocks.shape[0] // n, blocks.shape[1])
    mine = lax.optimization_barrier(jnp.sum(blocks.astype(jnp.float32), axis=0))
    out, at = [], 0
    for w in widths:
        out.append(mine[:, at : at + w])
        at += w
    return out


def scatter_packed(pieces, order=("core", "x", "z", "y"), direct=False):
    widths = [p.shape[1] for p in pieces]
    packed = jnp.concatenate(pieces, axis=1).astype(jnp.bfloat16)
    sizes = [lax.axis_size(a) for a in AXES]
    count = sizes[0] * sizes[1] * sizes[2] * sizes[3]
    per = packed.shape[0] // count
    blocks = packed.reshape(sizes + [per, packed.shape[1]])
    blocks = blocks.transpose([AXES.index(a) for a in order] + [4, 5])
    blocks = blocks.reshape(packed.shape)
    for axis in order:
        if direct:
            size = lax.axis_size(axis)
            got = lax.all_to_all(blocks, axis, 0, 0, tiled=True)
            got = got.reshape(size, got.shape[0] // size, got.shape[1])
            blocks = jnp.sum(got.astype(jnp.float32), axis=0).astype(jnp.bfloat16)
        else:
            blocks = lax.psum_scatter(blocks, axis, scatter_dimension=0, tiled=True)
    mine = lax.optimization_barrier(blocks).astype(jnp.float32)
    out, at = [], 0
    for w in widths:
        out.append(mine[:, at : at + w])
        at += w
    return out


def per_device(
    hidden_in,
    norm1_gain,
    in_weight,
    conv_weight,
    out_weight,
    norm2_gain,
    gate_weight,
    up_weight,
    down_weight,
    segment_ids,
    cotangent,
):
    rows = hidden_in.shape[0]
    width = hidden_in.shape[1]
    per = in_weight.shape[0]
    n = lax.axis_size(AXES)
    down_rows = down_weight.shape[0]
    small = jnp.concatenate(
        [norm1_gain[:, None], norm2_gain[:, None], conv_weight], axis=1
    )
    n_small = small.shape[1]
    w_in, w_out, small_full, w_gate, w_up, w_down_packed = gather_packed(
        [
            in_weight,
            out_weight,
            pad_cols(small),
            gate_weight,
            up_weight,
            down_weight.reshape(per, -1),
        ]
    )
    w_down = w_down_packed.reshape(n * down_rows, width)
    gain1 = small_full[:, 0]
    gain2 = small_full[:, 1]
    w_conv = small_full[:, 2 : 2 + CONV]

    xf = hidden_in.astype(jnp.float32)
    s1 = rms_scale(xf)
    h = (xf * s1 * gain1.astype(jnp.float32)).astype(jnp.bfloat16)
    proj = jnp.dot(h, w_in, preferred_element_type=jnp.float32)
    bgate = proj[:, :width]
    cgate = proj[:, width : 2 * width]
    xv = proj[:, 2 * width :]
    bx = (bgate * xv).astype(jnp.bfloat16)
    prev_rows, prev_ids = shifted(
        (bx[rows - 2 :], segment_ids[rows - 2 :].astype(jnp.bfloat16)), AXES, 1
    )
    ext_bx = jnp.concatenate([prev_rows, bx], axis=0).astype(jnp.float32)
    ext_ids = jnp.concatenate([prev_ids.astype(jnp.int32), segment_ids], axis=0)
    taps = w_conv.astype(jnp.float32)
    masks = [
        (ext_ids[2 - k : 2 - k + rows] == segment_ids).astype(jnp.float32)[:, None]
        for k in range(CONV)
    ]
    conv_out = jnp.zeros((rows, width), jnp.float32)
    for k in range(CONV):
        conv_out = conv_out + taps[:, k] * masks[k] * ext_bx[2 - k : 2 - k + rows]
    y = (cgate * conv_out).astype(jnp.bfloat16)
    resid = xf + jnp.dot(y, w_out, preferred_element_type=jnp.float32)
    s2 = rms_scale(resid)
    gain2f = gain2.astype(jnp.float32)
    h2 = (resid * s2 * gain2f).astype(jnp.bfloat16)
    a = jnp.dot(h2, w_gate, preferred_element_type=jnp.float32)
    b = jnp.dot(h2, w_up, preferred_element_type=jnp.float32)
    sig = jax.nn.sigmoid(a)
    act = a * sig
    z = (act * b).astype(jnp.bfloat16)
    block_out = (resid + jnp.dot(z, w_down, preferred_element_type=jnp.float32)).astype(
        jnp.bfloat16
    )

    dz = lax.dot_general(
        cotangent, w_down, (((1,), (1,)), ((), ())), preferred_element_type=jnp.float32
    )
    da = (dz * b * sig * (1.0 + a * (1.0 - sig))).astype(jnp.bfloat16)
    db = (dz * act).astype(jnp.bfloat16)
    g_down = lax.dot_general(
        z, cotangent, (((0,), (0,)), ((), ())), preferred_element_type=jnp.float32
    )
    g_gate = lax.dot_general(h2, da, (((0,), (0,)), ((), ())), preferred_element_type=jnp.float32)
    g_up = lax.dot_general(h2, db, (((0,), (0,)), ((), ())), preferred_element_type=jnp.float32)
    own_gate, own_up, own_down = scatter_packed(
        [g_gate, g_up, g_down.reshape(n * per, -1)]
    )
    dh2 = lax.dot_general(da, w_gate, (((1,), (1,)), ((), ())), preferred_element_type=jnp.float32)
    dh2 = dh2 + lax.dot_general(
        db, w_up, (((1,), (1,)), ((), ())), preferred_element_type=jnp.float32
    )
    g_gain2 = jnp.sum(dh2 * resid * s2, axis=0)
    dn2 = dh2 * gain2f
    d_resid = (
        cotangent.astype(jnp.float32)
        + s2 * dn2
        - resid * (s2 * s2 * s2) * jnp.mean(dn2 * resid, axis=-1, keepdims=True)
    )
    d_out = d_resid.astype(jnp.bfloat16)
    g_out = lax.dot_general(y, d_out, (((0,), (0,)), ((), ())), preferred_element_type=jnp.float32)
    dy = lax.dot_general(d_out, w_out, (((1,), (1,)), ((), ())), preferred_element_type=jnp.float32)
    d_cgate = dy * conv_out
    d_conv = dy * cgate
    d_ext = jnp.zeros((rows + 2, width), jnp.float32)
    tap_cols = []
    for k in range(CONV):
        term = d_conv * masks[k]
        d_ext = d_ext + jnp.pad(taps[:, k] * term, ((2 - k, k), (0, 0)))
        tap_cols.append(jnp.sum(term * ext_bx[2 - k : 2 - k + rows], axis=0))
    g_conv = jnp.stack(tap_cols, axis=1)
    returned = shifted(d_ext[:2], AXES, -1)
    d_bx = d_ext[2:] + jnp.pad(returned, ((rows - 2, 0), (0, 0)))
    d_proj = jnp.concatenate([d_bx * xv, d_cgate, d_bx * bgate], axis=1).astype(jnp.bfloat16)
    g_in = lax.dot_general(h, d_proj, (((0,), (0,)), ((), ())), preferred_element_type=jnp.float32)
    dh = lax.dot_general(d_proj, w_in, (((1,), (1,)), ((), ())), preferred_element_type=jnp.float32)
    g_gain1 = jnp.sum(dh * xf * s1, axis=0)
    dn1 = dh * gain1.astype(jnp.float32)
    input_grad = (
        d_resid + s1 * dn1 - xf * (s1 * s1 * s1) * jnp.mean(dn1 * xf, axis=-1, keepdims=True)
    )
    g_small = jnp.concatenate([g_gain1[:, None], g_gain2[:, None], g_conv], axis=1)
    own_in, own_out = scatter_packed(
        [g_in, g_out], order=("core", "y", "x", "z"), direct=True
    )
    (own_small,) = exchange_packed([pad_cols(g_small)])
    return (
        block_out,
        input_grad,
        own_small[:, 0],
        own_in,
        own_small[:, 2 : 2 + CONV],
        own_out,
        own_small[:, 1],
        own_gate,
        own_up,
        own_down.reshape(down_rows, width),
    )


def solution(mesh):
    torus = jax.sharding.Mesh(mesh.devices.reshape(4, 4, 4, 2), AXES)
    return jax.shard_map(
        per_device,
        mesh=torus,
        in_specs=(
            P(FSDP, None),
            P(FSDP),
            P(FSDP, None),
            P(FSDP, None),
            P(FSDP, None),
            P(FSDP),
            P(FSDP, None),
            P(FSDP, None),
            P(FSDP, None),
            P(FSDP),
            P(FSDP, None),
        ),
        out_specs=(
            P(FSDP, None),
            P(FSDP, None),
            P(FSDP),
            P(FSDP, None),
            P(FSDP, None),
            P(FSDP, None),
            P(FSDP),
            P(FSDP, None),
            P(FSDP, None),
            P(FSDP, None),
        ),
        check_vma=False,
    )
```

```python
import jax
import jax.numpy as jnp
from jax import lax
from jax.experimental import pallas as pl
from jax.experimental.pallas import tpu as pltpu
from jax.sharding import PartitionSpec as P

CONV = 3
EPS = 1e-05
LANE = 256


def shifted(value, axis, by):
    size = lax.axis_size(axis)
    pairs = [(i, i + by) for i in range(size) if 0 <= i + by < size]
    return lax.ppermute(value, axis, pairs)


def rms_scale(values):
    return lax.rsqrt(jnp.mean(values * values, axis=-1, keepdims=True) + EPS)


def pad_cols(x):
    extra = (-x.shape[1]) % LANE
    return jnp.pad(x, ((0, 0), (0, extra))) if extra else x


def gather_packed(pieces):
    widths = [p.shape[1] for p in pieces]
    packed = jnp.concatenate(pieces, axis=1)
    full = lax.all_gather(packed, AXES, axis=0, tiled=True)
    out, at = [], 0
    for w in widths:
        out.append(full[:, at : at + w])
        at += w
    return out


AXES = ("y", "z", "x", "core")
FSDP = AXES


def exchange_packed(pieces, dtype=jnp.float32):
    widths = [p.shape[1] for p in pieces]
    packed = jnp.concatenate(pieces, axis=1)
    n = lax.axis_size(AXES)
    blocks = lax.all_to_all(packed.astype(dtype), AXES, 0, 0, tiled=True)
    blocks = blocks.reshape(n, blocks.shape[0] // n, blocks.shape[1])
    mine = lax.optimization_barrier(jnp.sum(blocks.astype(jnp.float32), axis=0))
    out, at = [], 0
    for w in widths:
        out.append(mine[:, at : at + w])
        at += w
    return out


def pair_kernel(x_ref, o_ref, send_sem, recv_sem):
    other = 1 - lax.axis_index("core")
    partner = (lax.axis_index("y"), lax.axis_index("z"), lax.axis_index("x"), other)
    barrier = pltpu.get_barrier_semaphore()
    pl.semaphore_signal(
        barrier, inc=1, device_id=partner, device_id_type=pl.DeviceIdType.MESH
    )
    pl.semaphore_wait(barrier, 1)
    copy = pltpu.make_async_remote_copy(
        src_ref=x_ref.at[other],
        dst_ref=o_ref,
        send_sem=send_sem,
        recv_sem=recv_sem,
        device_id=partner,
        device_id_type=pl.DeviceIdType.MESH,
    )
    copy.start()
    copy.wait()


def pair_exchange(blocks, collective_id):
    halves = blocks.reshape(2, blocks.shape[0] // 2, blocks.shape[1])
    received = pl.pallas_call(
        pair_kernel,
        out_shape=jax.ShapeDtypeStruct(halves.shape[1:], halves.dtype),
        in_specs=[pl.BlockSpec(memory_space=pl.ANY)],
        out_specs=pl.BlockSpec(memory_space=pl.ANY),
        scratch_shapes=[pltpu.SemaphoreType.DMA(()), pltpu.SemaphoreType.DMA(())],
        compiler_params=pltpu.CompilerParams(
            collective_id=collective_id, has_side_effects=True
        ),
    )(halves)
    own = lax.dynamic_index_in_dim(halves, lax.axis_index("core"), 0, keepdims=False)
    return (own.astype(jnp.float32) + received.astype(jnp.float32)).astype(jnp.bfloat16)


def scatter_packed(pieces, order=("core", "x", "z", "y"), direct=False, collective_id=0):
    widths = [p.shape[1] for p in pieces]
    packed = jnp.concatenate(pieces, axis=1).astype(jnp.bfloat16)
    sizes = [lax.axis_size(a) for a in AXES]
    count = sizes[0] * sizes[1] * sizes[2] * sizes[3]
    per = packed.shape[0] // count
    blocks = packed.reshape(sizes + [per, packed.shape[1]])
    blocks = blocks.transpose([AXES.index(a) for a in order] + [4, 5])
    blocks = blocks.reshape(packed.shape)
    for axis in order:
        if direct and axis == "core":
            blocks = pair_exchange(blocks, collective_id)
        elif direct:
            size = lax.axis_size(axis)
            got = lax.all_to_all(blocks, axis, 0, 0, tiled=True)
            got = got.reshape(size, got.shape[0] // size, got.shape[1])
            blocks = jnp.sum(got.astype(jnp.float32), axis=0).astype(jnp.bfloat16)
        else:
            blocks = lax.psum_scatter(blocks, axis, scatter_dimension=0, tiled=True)
    mine = lax.optimization_barrier(blocks).astype(jnp.float32)
    out, at = [], 0
    for w in widths:
        out.append(mine[:, at : at + w])
        at += w
    return out


def per_device(
    hidden_in,
    norm1_gain,
    in_weight,
    conv_weight,
    out_weight,
    norm2_gain,
    gate_weight,
    up_weight,
    down_weight,
    segment_ids,
    cotangent,
):
    rows = hidden_in.shape[0]
    width = hidden_in.shape[1]
    per = in_weight.shape[0]
    n = lax.axis_size(AXES)
    down_rows = down_weight.shape[0]
    small = jnp.concatenate(
        [norm1_gain[:, None], norm2_gain[:, None], conv_weight], axis=1
    )
    n_small = small.shape[1]
    w_in, w_out, small_full, w_gate, w_up, w_down_packed = gather_packed(
        [
            in_weight,
            out_weight,
            pad_cols(small),
            gate_weight,
            up_weight,
            down_weight.reshape(per, -1),
        ]
    )
    w_down = w_down_packed.reshape(n * down_rows, width)
    gain1 = small_full[:, 0]
    gain2 = small_full[:, 1]
    w_conv = small_full[:, 2 : 2 + CONV]

    xf = hidden_in.astype(jnp.float32)
    s1 = rms_scale(xf)
    h = (xf * s1 * gain1.astype(jnp.float32)).astype(jnp.bfloat16)
    proj = jnp.dot(h, w_in, preferred_element_type=jnp.float32)
    bgate = proj[:, :width]
    cgate = proj[:, width : 2 * width]
    xv = proj[:, 2 * width :]
    bx = (bgate * xv).astype(jnp.bfloat16)
    prev_rows, prev_ids = shifted(
        (bx[rows - 2 :], segment_ids[rows - 2 :].astype(jnp.bfloat16)), AXES, 1
    )
    ext_bx = jnp.concatenate([prev_rows, bx], axis=0).astype(jnp.float32)
    ext_ids = jnp.concatenate([prev_ids.astype(jnp.int32), segment_ids], axis=0)
    taps = w_conv.astype(jnp.float32)
    masks = [
        (ext_ids[2 - k : 2 - k + rows] == segment_ids).astype(jnp.float32)[:, None]
        for k in range(CONV)
    ]
    conv_out = jnp.zeros((rows, width), jnp.float32)
    for k in range(CONV):
        conv_out = conv_out + taps[:, k] * masks[k] * ext_bx[2 - k : 2 - k + rows]
    y = (cgate * conv_out).astype(jnp.bfloat16)
    resid = xf + jnp.dot(y, w_out, preferred_element_type=jnp.float32)
    s2 = rms_scale(resid)
    gain2f = gain2.astype(jnp.float32)
    h2 = (resid * s2 * gain2f).astype(jnp.bfloat16)
    a = jnp.dot(h2, w_gate, preferred_element_type=jnp.float32)
    b = jnp.dot(h2, w_up, preferred_element_type=jnp.float32)
    sig = jax.nn.sigmoid(a)
    act = a * sig
    z = (act * b).astype(jnp.bfloat16)
    block_out = (resid + jnp.dot(z, w_down, preferred_element_type=jnp.float32)).astype(
        jnp.bfloat16
    )

    dz = lax.dot_general(
        cotangent, w_down, (((1,), (1,)), ((), ())), preferred_element_type=jnp.float32
    )
    da = (dz * b * sig * (1.0 + a * (1.0 - sig))).astype(jnp.bfloat16)
    db = (dz * act).astype(jnp.bfloat16)
    g_down = lax.dot_general(
        z, cotangent, (((0,), (0,)), ((), ())), preferred_element_type=jnp.float32
    )
    g_gate = lax.dot_general(h2, da, (((0,), (0,)), ((), ())), preferred_element_type=jnp.float32)
    g_up = lax.dot_general(h2, db, (((0,), (0,)), ((), ())), preferred_element_type=jnp.float32)
    own_gate, own_up = scatter_packed([g_gate, g_up])
    (own_down,) = scatter_packed(
        [g_down.reshape(n * per, -1)],
        order=("core", "z", "y", "x"),
        direct=True,
        collective_id=1,
    )
    dh2 = lax.dot_general(da, w_gate, (((1,), (1,)), ((), ())), preferred_element_type=jnp.float32)
    dh2 = dh2 + lax.dot_general(
        db, w_up, (((1,), (1,)), ((), ())), preferred_element_type=jnp.float32
    )
    g_gain2 = jnp.sum(dh2 * resid * s2, axis=0)
    dn2 = dh2 * gain2f
    d_resid = (
        cotangent.astype(jnp.float32)
        + s2 * dn2
        - resid * (s2 * s2 * s2) * jnp.mean(dn2 * resid, axis=-1, keepdims=True)
    )
    d_out = d_resid.astype(jnp.bfloat16)
    g_out = lax.dot_general(y, d_out, (((0,), (0,)), ((), ())), preferred_element_type=jnp.float32)
    dy = lax.dot_general(d_out, w_out, (((1,), (1,)), ((), ())), preferred_element_type=jnp.float32)
    d_cgate = dy * conv_out
    d_conv = dy * cgate
    d_ext = jnp.zeros((rows + 2, width), jnp.float32)
    tap_cols = []
    for k in range(CONV):
        term = d_conv * masks[k]
        d_ext = d_ext + jnp.pad(taps[:, k] * term, ((2 - k, k), (0, 0)))
        tap_cols.append(jnp.sum(term * ext_bx[2 - k : 2 - k + rows], axis=0))
    g_conv = jnp.stack(tap_cols, axis=1)
    returned = shifted(d_ext[:2], AXES, -1)
    d_bx = d_ext[2:] + jnp.pad(returned, ((rows - 2, 0), (0, 0)))
    d_proj = jnp.concatenate([d_bx * xv, d_cgate, d_bx * bgate], axis=1).astype(jnp.bfloat16)
    g_in = lax.dot_general(h, d_proj, (((0,), (0,)), ((), ())), preferred_element_type=jnp.float32)
    dh = lax.dot_general(d_proj, w_in, (((1,), (1,)), ((), ())), preferred_element_type=jnp.float32)
    g_gain1 = jnp.sum(dh * xf * s1, axis=0)
    dn1 = dh * gain1.astype(jnp.float32)
    input_grad = (
        d_resid + s1 * dn1 - xf * (s1 * s1 * s1) * jnp.mean(dn1 * xf, axis=-1, keepdims=True)
    )
    g_small = jnp.concatenate([g_gain1[:, None], g_gain2[:, None], g_conv], axis=1)
    own_in, own_out = scatter_packed(
        [g_in, g_out], order=("core", "y", "x", "z"), direct=True, collective_id=2
    )
    (own_small,) = exchange_packed([pad_cols(g_small)])
    return (
        block_out,
        input_grad,
        own_small[:, 0],
        own_in,
        own_small[:, 2 : 2 + CONV],
        own_out,
        own_small[:, 1],
        own_gate,
        own_up,
        own_down.reshape(down_rows, width),
    )


def solution(mesh):
    torus = jax.sharding.Mesh(mesh.devices.reshape(4, 4, 4, 2), AXES)
    return jax.shard_map(
        per_device,
        mesh=torus,
        in_specs=(
            P(FSDP, None),
            P(FSDP),
            P(FSDP, None),
            P(FSDP, None),
            P(FSDP, None),
            P(FSDP),
            P(FSDP, None),
            P(FSDP, None),
            P(FSDP, None),
            P(FSDP),
            P(FSDP, None),
        ),
        out_specs=(
            P(FSDP, None),
            P(FSDP, None),
            P(FSDP),
            P(FSDP, None),
            P(FSDP, None),
            P(FSDP, None),
            P(FSDP),
            P(FSDP, None),
            P(FSDP, None),
            P(FSDP, None),
        ),
        check_vma=False,
    )
```

```python
import jax
import jax.numpy as jnp
from jax import lax
from jax.experimental import pallas as pl
from jax.experimental.pallas import tpu as pltpu
from jax.sharding import PartitionSpec as P

CONV = 3
EPS = 1e-05
LANE = 256


def shifted(value, axis, by):
    size = lax.axis_size(axis)
    pairs = [(i, i + by) for i in range(size) if 0 <= i + by < size]
    return lax.ppermute(value, axis, pairs)


def rms_scale(values):
    return lax.rsqrt(jnp.mean(values * values, axis=-1, keepdims=True) + EPS)


def pad_cols(x):
    extra = (-x.shape[1]) % LANE
    return jnp.pad(x, ((0, 0), (0, extra))) if extra else x


def gather_packed(pieces):
    widths = [p.shape[1] for p in pieces]
    packed = jnp.concatenate(pieces, axis=1)
    full = lax.all_gather(packed, AXES, axis=0, tiled=True)
    out, at = [], 0
    for w in widths:
        out.append(full[:, at : at + w])
        at += w
    return out


AXES = ("y", "z", "x", "core")
FSDP = AXES


def exchange_packed(pieces, dtype=jnp.float32):
    widths = [p.shape[1] for p in pieces]
    packed = jnp.concatenate(pieces, axis=1)
    n = lax.axis_size(AXES)
    blocks = lax.all_to_all(packed.astype(dtype), AXES, 0, 0, tiled=True)
    blocks = blocks.reshape(n, blocks.shape[0] // n, blocks.shape[1])
    mine = lax.optimization_barrier(jnp.sum(blocks.astype(jnp.float32), axis=0))
    out, at = [], 0
    for w in widths:
        out.append(mine[:, at : at + w])
        at += w
    return out


def pair_kernel(x_ref, o_ref, send_sem, recv_sem):
    other = 1 - lax.axis_index("core")
    partner = (lax.axis_index("y"), lax.axis_index("z"), lax.axis_index("x"), other)
    barrier = pltpu.get_barrier_semaphore()
    pl.semaphore_signal(
        barrier, inc=1, device_id=partner, device_id_type=pl.DeviceIdType.MESH
    )
    pl.semaphore_wait(barrier, 1)
    copy = pltpu.make_async_remote_copy(
        src_ref=x_ref.at[other],
        dst_ref=o_ref,
        send_sem=send_sem,
        recv_sem=recv_sem,
        device_id=partner,
        device_id_type=pl.DeviceIdType.MESH,
    )
    copy.start()
    copy.wait()


def pair_exchange(blocks, collective_id):
    halves = blocks.reshape(2, blocks.shape[0] // 2, blocks.shape[1])
    received = pl.pallas_call(
        pair_kernel,
        out_shape=jax.ShapeDtypeStruct(halves.shape[1:], halves.dtype),
        in_specs=[pl.BlockSpec(memory_space=pl.ANY)],
        out_specs=pl.BlockSpec(memory_space=pl.ANY),
        scratch_shapes=[pltpu.SemaphoreType.DMA(()), pltpu.SemaphoreType.DMA(())],
        compiler_params=pltpu.CompilerParams(
            collective_id=collective_id, has_side_effects=True
        ),
    )(halves)
    own = lax.dynamic_index_in_dim(halves, lax.axis_index("core"), 0, keepdims=False)
    return (own.astype(jnp.float32) + received.astype(jnp.float32)).astype(jnp.bfloat16)


def scatter_packed(pieces, order=("core", "x", "z", "y"), direct=False, collective_id=0):
    widths = [p.shape[1] for p in pieces]
    packed = jnp.concatenate(pieces, axis=1).astype(jnp.bfloat16)
    sizes = [lax.axis_size(a) for a in AXES]
    count = sizes[0] * sizes[1] * sizes[2] * sizes[3]
    per = packed.shape[0] // count
    blocks = packed.reshape(sizes + [per, packed.shape[1]])
    blocks = blocks.transpose([AXES.index(a) for a in order] + [4, 5])
    blocks = blocks.reshape(packed.shape)
    for axis in order:
        if axis == "core":
            blocks = pair_exchange(blocks, collective_id)
        elif direct:
            size = lax.axis_size(axis)
            got = lax.all_to_all(blocks, axis, 0, 0, tiled=True)
            got = got.reshape(size, got.shape[0] // size, got.shape[1])
            blocks = jnp.sum(got.astype(jnp.float32), axis=0).astype(jnp.bfloat16)
        else:
            blocks = lax.psum_scatter(blocks, axis, scatter_dimension=0, tiled=True)
    mine = lax.optimization_barrier(blocks).astype(jnp.float32)
    out, at = [], 0
    for w in widths:
        out.append(mine[:, at : at + w])
        at += w
    return out


def per_device(
    hidden_in,
    norm1_gain,
    in_weight,
    conv_weight,
    out_weight,
    norm2_gain,
    gate_weight,
    up_weight,
    down_weight,
    segment_ids,
    cotangent,
):
    rows = hidden_in.shape[0]
    width = hidden_in.shape[1]
    per = in_weight.shape[0]
    n = lax.axis_size(AXES)
    down_rows = down_weight.shape[0]
    small = jnp.concatenate(
        [norm1_gain[:, None], norm2_gain[:, None], conv_weight], axis=1
    )
    n_small = small.shape[1]
    w_in, w_out, small_full, w_gate, w_up, w_down_packed = gather_packed(
        [
            in_weight,
            out_weight,
            pad_cols(small),
            gate_weight,
            up_weight,
            down_weight.reshape(per, -1),
        ]
    )
    w_down = w_down_packed.reshape(n * down_rows, width)
    gain1 = small_full[:, 0]
    gain2 = small_full[:, 1]
    w_conv = small_full[:, 2 : 2 + CONV]

    xf = hidden_in.astype(jnp.float32)
    s1 = rms_scale(xf)
    h = (xf * s1 * gain1.astype(jnp.float32)).astype(jnp.bfloat16)
    proj = jnp.dot(h, w_in, preferred_element_type=jnp.float32)
    bgate = proj[:, :width]
    cgate = proj[:, width : 2 * width]
    xv = proj[:, 2 * width :]
    bx = (bgate * xv).astype(jnp.bfloat16)
    prev_rows, prev_ids = shifted(
        (bx[rows - 2 :], segment_ids[rows - 2 :].astype(jnp.bfloat16)), AXES, 1
    )
    ext_bx = jnp.concatenate([prev_rows, bx], axis=0).astype(jnp.float32)
    ext_ids = jnp.concatenate([prev_ids.astype(jnp.int32), segment_ids], axis=0)
    taps = w_conv.astype(jnp.float32)
    masks = [
        (ext_ids[2 - k : 2 - k + rows] == segment_ids).astype(jnp.float32)[:, None]
        for k in range(CONV)
    ]
    conv_out = jnp.zeros((rows, width), jnp.float32)
    for k in range(CONV):
        conv_out = conv_out + taps[:, k] * masks[k] * ext_bx[2 - k : 2 - k + rows]
    y = (cgate * conv_out).astype(jnp.bfloat16)
    resid = xf + jnp.dot(y, w_out, preferred_element_type=jnp.float32)
    s2 = rms_scale(resid)
    gain2f = gain2.astype(jnp.float32)
    h2 = (resid * s2 * gain2f).astype(jnp.bfloat16)
    a = jnp.dot(h2, w_gate, preferred_element_type=jnp.float32)
    b = jnp.dot(h2, w_up, preferred_element_type=jnp.float32)
    sig = jax.nn.sigmoid(a)
    act = a * sig
    z = (act * b).astype(jnp.bfloat16)
    block_out = (resid + jnp.dot(z, w_down, preferred_element_type=jnp.float32)).astype(
        jnp.bfloat16
    )

    dz = lax.dot_general(
        cotangent, w_down, (((1,), (1,)), ((), ())), preferred_element_type=jnp.float32
    )
    da = (dz * b * sig * (1.0 + a * (1.0 - sig))).astype(jnp.bfloat16)
    db = (dz * act).astype(jnp.bfloat16)
    g_down = lax.dot_general(
        z, cotangent, (((0,), (0,)), ((), ())), preferred_element_type=jnp.float32
    )
    g_gate = lax.dot_general(h2, da, (((0,), (0,)), ((), ())), preferred_element_type=jnp.float32)
    g_up = lax.dot_general(h2, db, (((0,), (0,)), ((), ())), preferred_element_type=jnp.float32)
    own_gate, own_up = scatter_packed([g_gate, g_up])
    (own_down,) = scatter_packed(
        [g_down.reshape(n * per, -1)],
        order=("core", "z", "y", "x"),
        direct=True,
        collective_id=1,
    )
    dh2 = lax.dot_general(da, w_gate, (((1,), (1,)), ((), ())), preferred_element_type=jnp.float32)
    dh2 = dh2 + lax.dot_general(
        db, w_up, (((1,), (1,)), ((), ())), preferred_element_type=jnp.float32
    )
    g_gain2 = jnp.sum(dh2 * resid * s2, axis=0)
    dn2 = dh2 * gain2f
    d_resid = (
        cotangent.astype(jnp.float32)
        + s2 * dn2
        - resid * (s2 * s2 * s2) * jnp.mean(dn2 * resid, axis=-1, keepdims=True)
    )
    d_out = d_resid.astype(jnp.bfloat16)
    g_out = lax.dot_general(y, d_out, (((0,), (0,)), ((), ())), preferred_element_type=jnp.float32)
    dy = lax.dot_general(d_out, w_out, (((1,), (1,)), ((), ())), preferred_element_type=jnp.float32)
    d_cgate = dy * conv_out
    d_conv = dy * cgate
    d_ext = jnp.zeros((rows + 2, width), jnp.float32)
    tap_cols = []
    for k in range(CONV):
        term = d_conv * masks[k]
        d_ext = d_ext + jnp.pad(taps[:, k] * term, ((2 - k, k), (0, 0)))
        tap_cols.append(jnp.sum(term * ext_bx[2 - k : 2 - k + rows], axis=0))
    g_conv = jnp.stack(tap_cols, axis=1)
    returned = shifted(d_ext[:2], AXES, -1)
    d_bx = d_ext[2:] + jnp.pad(returned, ((rows - 2, 0), (0, 0)))
    d_proj = jnp.concatenate([d_bx * xv, d_cgate, d_bx * bgate], axis=1).astype(jnp.bfloat16)
    g_in = lax.dot_general(h, d_proj, (((0,), (0,)), ((), ())), preferred_element_type=jnp.float32)
    dh = lax.dot_general(d_proj, w_in, (((1,), (1,)), ((), ())), preferred_element_type=jnp.float32)
    g_gain1 = jnp.sum(dh * xf * s1, axis=0)
    dn1 = dh * gain1.astype(jnp.float32)
    input_grad = (
        d_resid + s1 * dn1 - xf * (s1 * s1 * s1) * jnp.mean(dn1 * xf, axis=-1, keepdims=True)
    )
    g_small = jnp.concatenate([g_gain1[:, None], g_gain2[:, None], g_conv], axis=1)
    own_in, own_out = scatter_packed(
        [g_in, g_out], order=("core", "y", "x", "z"), direct=True, collective_id=2
    )
    (own_small,) = exchange_packed([pad_cols(g_small)])
    return (
        block_out,
        input_grad,
        own_small[:, 0],
        own_in,
        own_small[:, 2 : 2 + CONV],
        own_out,
        own_small[:, 1],
        own_gate,
        own_up,
        own_down.reshape(down_rows, width),
    )


def solution(mesh):
    torus = jax.sharding.Mesh(mesh.devices.reshape(4, 4, 4, 2), AXES)
    return jax.shard_map(
        per_device,
        mesh=torus,
        in_specs=(
            P(FSDP, None),
            P(FSDP),
            P(FSDP, None),
            P(FSDP, None),
            P(FSDP, None),
            P(FSDP),
            P(FSDP, None),
            P(FSDP, None),
            P(FSDP, None),
            P(FSDP),
            P(FSDP, None),
        ),
        out_specs=(
            P(FSDP, None),
            P(FSDP, None),
            P(FSDP),
            P(FSDP, None),
            P(FSDP, None),
            P(FSDP, None),
            P(FSDP),
            P(FSDP, None),
            P(FSDP, None),
            P(FSDP, None),
        ),
        check_vma=False,
    )
```

```python
import jax
import jax.numpy as jnp
from jax import lax
from jax.experimental import pallas as pl
from jax.experimental.pallas import tpu as pltpu
from jax.sharding import PartitionSpec as P

CONV = 3
EPS = 1e-05
LANE = 256


def shifted(value, axis, by):
    size = lax.axis_size(axis)
    pairs = [(i, i + by) for i in range(size) if 0 <= i + by < size]
    return lax.ppermute(value, axis, pairs)


def rms_scale(values):
    return lax.rsqrt(jnp.mean(values * values, axis=-1, keepdims=True) + EPS)


def pad_cols(x):
    extra = (-x.shape[1]) % LANE
    return jnp.pad(x, ((0, 0), (0, extra))) if extra else x


def gather_packed(pieces):
    widths = [p.shape[1] for p in pieces]
    packed = jnp.concatenate(pieces, axis=1)
    full = lax.all_gather(packed, AXES, axis=0, tiled=True)
    out, at = [], 0
    for w in widths:
        out.append(full[:, at : at + w])
        at += w
    return out


AXES = ("y", "z", "x", "core")
FSDP = AXES
ORDER_UP = ("core", "x", "z", "y")
ORDER_DOWN = ("core", "z", "y", "x")
ORDER_IN = ("core", "y", "x", "z")


def exchange_packed(pieces, dtype=jnp.float32):
    widths = [p.shape[1] for p in pieces]
    packed = jnp.concatenate(pieces, axis=1)
    n = lax.axis_size(AXES)
    blocks = lax.all_to_all(packed.astype(dtype), AXES, 0, 0, tiled=True)
    blocks = blocks.reshape(n, blocks.shape[0] // n, blocks.shape[1])
    mine = lax.optimization_barrier(jnp.sum(blocks.astype(jnp.float32), axis=0))
    out, at = [], 0
    for w in widths:
        out.append(mine[:, at : at + w])
        at += w
    return out


def pair_kernel(x_ref, o_ref, send_sem, recv_sem):
    other = 1 - lax.axis_index("core")
    partner = (lax.axis_index("y"), lax.axis_index("z"), lax.axis_index("x"), other)
    barrier = pltpu.get_barrier_semaphore()
    pl.semaphore_signal(
        barrier, inc=1, device_id=partner, device_id_type=pl.DeviceIdType.MESH
    )
    pl.semaphore_wait(barrier, 1)
    copy = pltpu.make_async_remote_copy(
        src_ref=x_ref.at[other],
        dst_ref=o_ref,
        send_sem=send_sem,
        recv_sem=recv_sem,
        device_id=partner,
        device_id_type=pl.DeviceIdType.MESH,
    )
    copy.start()
    copy.wait()


def pair_exchange(blocks, collective_id):
    halves = blocks.reshape(2, blocks.shape[0] // 2, blocks.shape[1])
    received = pl.pallas_call(
        pair_kernel,
        out_shape=jax.ShapeDtypeStruct(halves.shape[1:], halves.dtype),
        in_specs=[pl.BlockSpec(memory_space=pl.ANY)],
        out_specs=pl.BlockSpec(memory_space=pl.ANY),
        scratch_shapes=[pltpu.SemaphoreType.DMA(()), pltpu.SemaphoreType.DMA(())],
        compiler_params=pltpu.CompilerParams(
            collective_id=collective_id, has_side_effects=True
        ),
    )(halves)
    own = lax.dynamic_index_in_dim(halves, lax.axis_index("core"), 0, keepdims=False)
    return (own.astype(jnp.float32) + received.astype(jnp.float32)).astype(jnp.bfloat16)


def in_stage_order(values, order):
    sizes = [lax.axis_size(a) for a in AXES]
    group = values.shape[1] // (sizes[0] * sizes[1] * sizes[2] * sizes[3])
    grid = values.reshape([values.shape[0]] + sizes + [group])
    grid = grid.transpose([0] + [1 + AXES.index(a) for a in order] + [5])
    return grid.reshape(values.shape)


def scatter_packed(pieces, order=("core", "x", "z", "y"), direct=False, collective_id=0):
    widths = [p.shape[1] for p in pieces]
    packed = jnp.concatenate(pieces, axis=1).astype(jnp.bfloat16)
    sizes = [lax.axis_size(a) for a in AXES]
    count = sizes[0] * sizes[1] * sizes[2] * sizes[3]
    per = packed.shape[0] // count
    blocks = packed
    for axis in order:
        if axis == "core":
            blocks = pair_exchange(blocks, collective_id)
        elif direct:
            size = lax.axis_size(axis)
            got = lax.all_to_all(blocks, axis, 0, 0, tiled=True)
            got = got.reshape(size, got.shape[0] // size, got.shape[1])
            blocks = jnp.sum(got.astype(jnp.float32), axis=0).astype(jnp.bfloat16)
        else:
            blocks = lax.psum_scatter(blocks, axis, scatter_dimension=0, tiled=True)
    mine = lax.optimization_barrier(blocks).astype(jnp.float32)
    out, at = [], 0
    for w in widths:
        out.append(mine[:, at : at + w])
        at += w
    return out


def per_device(
    hidden_in,
    norm1_gain,
    in_weight,
    conv_weight,
    out_weight,
    norm2_gain,
    gate_weight,
    up_weight,
    down_weight,
    segment_ids,
    cotangent,
):
    rows = hidden_in.shape[0]
    width = hidden_in.shape[1]
    per = in_weight.shape[0]
    n = lax.axis_size(AXES)
    down_rows = down_weight.shape[0]
    small = jnp.concatenate(
        [norm1_gain[:, None], norm2_gain[:, None], conv_weight], axis=1
    )
    n_small = small.shape[1]
    w_in, w_out, small_full, w_gate, w_up, w_down_packed = gather_packed(
        [
            in_weight,
            out_weight,
            pad_cols(small),
            gate_weight,
            up_weight,
            down_weight.reshape(per, -1),
        ]
    )
    w_down = w_down_packed.reshape(n * down_rows, width)
    gain1 = small_full[:, 0]
    gain2 = small_full[:, 1]
    w_conv = small_full[:, 2 : 2 + CONV]

    xf = hidden_in.astype(jnp.float32)
    s1 = rms_scale(xf)
    h = (xf * s1 * gain1.astype(jnp.float32)).astype(jnp.bfloat16)
    proj = jnp.dot(h, w_in, preferred_element_type=jnp.float32)
    bgate = proj[:, :width]
    cgate = proj[:, width : 2 * width]
    xv = proj[:, 2 * width :]
    bx = (bgate * xv).astype(jnp.bfloat16)
    prev_rows, prev_ids = shifted(
        (bx[rows - 2 :], segment_ids[rows - 2 :].astype(jnp.bfloat16)), AXES, 1
    )
    ext_bx = jnp.concatenate([prev_rows, bx], axis=0).astype(jnp.float32)
    ext_ids = jnp.concatenate([prev_ids.astype(jnp.int32), segment_ids], axis=0)
    taps = w_conv.astype(jnp.float32)
    masks = [
        (ext_ids[2 - k : 2 - k + rows] == segment_ids).astype(jnp.float32)[:, None]
        for k in range(CONV)
    ]
    conv_out = jnp.zeros((rows, width), jnp.float32)
    for k in range(CONV):
        conv_out = conv_out + taps[:, k] * masks[k] * ext_bx[2 - k : 2 - k + rows]
    y = (cgate * conv_out).astype(jnp.bfloat16)
    resid = xf + jnp.dot(y, w_out, preferred_element_type=jnp.float32)
    s2 = rms_scale(resid)
    gain2f = gain2.astype(jnp.float32)
    h2 = (resid * s2 * gain2f).astype(jnp.bfloat16)
    a = jnp.dot(h2, w_gate, preferred_element_type=jnp.float32)
    b = jnp.dot(h2, w_up, preferred_element_type=jnp.float32)
    sig = jax.nn.sigmoid(a)
    act = a * sig
    z = (act * b).astype(jnp.bfloat16)
    block_out = (resid + jnp.dot(z, w_down, preferred_element_type=jnp.float32)).astype(
        jnp.bfloat16
    )

    dz = lax.dot_general(
        cotangent, w_down, (((1,), (1,)), ((), ())), preferred_element_type=jnp.float32
    )
    da = (dz * b * sig * (1.0 + a * (1.0 - sig))).astype(jnp.bfloat16)
    db = (dz * act).astype(jnp.bfloat16)
    h2_up = in_stage_order(h2, ORDER_UP)
    g_down = lax.dot_general(
        in_stage_order(z, ORDER_DOWN),
        cotangent,
        (((0,), (0,)), ((), ())),
        preferred_element_type=jnp.bfloat16,
    )
    g_gate = lax.dot_general(
        h2_up, da, (((0,), (0,)), ((), ())), preferred_element_type=jnp.bfloat16
    )
    g_up = lax.dot_general(
        h2_up, db, (((0,), (0,)), ((), ())), preferred_element_type=jnp.bfloat16
    )
    own_gate, own_up = scatter_packed([g_gate, g_up], order=ORDER_UP)
    (own_down,) = scatter_packed(
        [g_down.reshape(n * per, -1)],
        order=ORDER_DOWN,
        direct=True,
        collective_id=1,
    )
    dh2 = lax.dot_general(da, w_gate, (((1,), (1,)), ((), ())), preferred_element_type=jnp.float32)
    dh2 = dh2 + lax.dot_general(
        db, w_up, (((1,), (1,)), ((), ())), preferred_element_type=jnp.float32
    )
    g_gain2 = jnp.sum(dh2 * resid * s2, axis=0)
    dn2 = dh2 * gain2f
    d_resid = (
        cotangent.astype(jnp.float32)
        + s2 * dn2
        - resid * (s2 * s2 * s2) * jnp.mean(dn2 * resid, axis=-1, keepdims=True)
    )
    d_out = d_resid.astype(jnp.bfloat16)
    g_out = lax.dot_general(
        in_stage_order(y, ORDER_IN),
        d_out,
        (((0,), (0,)), ((), ())),
        preferred_element_type=jnp.bfloat16,
    )
    dy = lax.dot_general(d_out, w_out, (((1,), (1,)), ((), ())), preferred_element_type=jnp.float32)
    d_cgate = dy * conv_out
    d_conv = dy * cgate
    d_ext = jnp.zeros((rows + 2, width), jnp.float32)
    tap_cols = []
    for k in range(CONV):
        term = d_conv * masks[k]
        d_ext = d_ext + jnp.pad(taps[:, k] * term, ((2 - k, k), (0, 0)))
        tap_cols.append(jnp.sum(term * ext_bx[2 - k : 2 - k + rows], axis=0))
    g_conv = jnp.stack(tap_cols, axis=1)
    returned = shifted(d_ext[:2], AXES, -1)
    d_bx = d_ext[2:] + jnp.pad(returned, ((rows - 2, 0), (0, 0)))
    d_proj = jnp.concatenate([d_bx * xv, d_cgate, d_bx * bgate], axis=1).astype(jnp.bfloat16)
    g_in = lax.dot_general(
        in_stage_order(h, ORDER_IN),
        d_proj,
        (((0,), (0,)), ((), ())),
        preferred_element_type=jnp.bfloat16,
    )
    dh = lax.dot_general(d_proj, w_in, (((1,), (1,)), ((), ())), preferred_element_type=jnp.float32)
    g_gain1 = jnp.sum(dh * xf * s1, axis=0)
    dn1 = dh * gain1.astype(jnp.float32)
    input_grad = (
        d_resid + s1 * dn1 - xf * (s1 * s1 * s1) * jnp.mean(dn1 * xf, axis=-1, keepdims=True)
    )
    g_small = jnp.concatenate([g_gain1[:, None], g_gain2[:, None], g_conv], axis=1)
    own_in, own_out = scatter_packed(
        [g_in, g_out], order=ORDER_IN, direct=True, collective_id=2
    )
    (own_small,) = exchange_packed([pad_cols(g_small)])
    return (
        block_out,
        input_grad,
        own_small[:, 0],
        own_in,
        own_small[:, 2 : 2 + CONV],
        own_out,
        own_small[:, 1],
        own_gate,
        own_up,
        own_down.reshape(down_rows, width),
    )


def solution(mesh):
    torus = jax.sharding.Mesh(mesh.devices.reshape(4, 4, 4, 2), AXES)
    return jax.shard_map(
        per_device,
        mesh=torus,
        in_specs=(
            P(FSDP, None),
            P(FSDP),
            P(FSDP, None),
            P(FSDP, None),
            P(FSDP, None),
            P(FSDP),
            P(FSDP, None),
            P(FSDP, None),
            P(FSDP, None),
            P(FSDP),
            P(FSDP, None),
        ),
        out_specs=(
            P(FSDP, None),
            P(FSDP, None),
            P(FSDP),
            P(FSDP, None),
            P(FSDP, None),
            P(FSDP, None),
            P(FSDP),
            P(FSDP, None),
            P(FSDP, None),
            P(FSDP, None),
        ),
        check_vma=False,
    )
```

```python
import jax
import jax.numpy as jnp
from jax import lax
from jax.experimental import pallas as pl
from jax.experimental.pallas import tpu as pltpu
from jax.sharding import PartitionSpec as P

CONV = 3
EPS = 1e-05
LANE = 256


def shifted(value, axis, by):
    size = lax.axis_size(axis)
    pairs = [(i, i + by) for i in range(size) if 0 <= i + by < size]
    return lax.ppermute(value, axis, pairs)


def rms_scale(values):
    return lax.rsqrt(jnp.mean(values * values, axis=-1, keepdims=True) + EPS)


def pad_cols(x):
    extra = (-x.shape[1]) % LANE
    return jnp.pad(x, ((0, 0), (0, extra))) if extra else x


def gather_packed(pieces):
    widths = [p.shape[1] for p in pieces]
    packed = jnp.concatenate(pieces, axis=1)
    full = lax.all_gather(packed, AXES, axis=0, tiled=True)
    out, at = [], 0
    for w in widths:
        out.append(full[:, at : at + w])
        at += w
    return out


AXES = ("y", "z", "x", "core")
FSDP = AXES
ORDER_UP = ("core", "x", "z", "y")
ORDER_DOWN = ("core", "z", "y", "x")
ORDER_IN = ("core", "y", "x", "z")


def exchange_packed(pieces, dtype=jnp.float32):
    widths = [p.shape[1] for p in pieces]
    packed = jnp.concatenate(pieces, axis=1)
    n = lax.axis_size(AXES)
    blocks = lax.all_to_all(packed.astype(dtype), AXES, 0, 0, tiled=True)
    blocks = blocks.reshape(n, blocks.shape[0] // n, blocks.shape[1])
    mine = lax.optimization_barrier(jnp.sum(blocks.astype(jnp.float32), axis=0))
    out, at = [], 0
    for w in widths:
        out.append(mine[:, at : at + w])
        at += w
    return out


def pair_kernel(x_ref, o_ref, send_sem, recv_sem):
    other = 1 - lax.axis_index("core")
    partner = (lax.axis_index("y"), lax.axis_index("z"), lax.axis_index("x"), other)
    barrier = pltpu.get_barrier_semaphore()
    pl.semaphore_signal(
        barrier, inc=1, device_id=partner, device_id_type=pl.DeviceIdType.MESH
    )
    pl.semaphore_wait(barrier, 1)
    copy = pltpu.make_async_remote_copy(
        src_ref=x_ref.at[other],
        dst_ref=o_ref,
        send_sem=send_sem,
        recv_sem=recv_sem,
        device_id=partner,
        device_id_type=pl.DeviceIdType.MESH,
    )
    copy.start()
    copy.wait()


def pair_exchange(blocks, collective_id):
    halves = blocks.reshape(2, blocks.shape[0] // 2, blocks.shape[1])
    received = pl.pallas_call(
        pair_kernel,
        out_shape=jax.ShapeDtypeStruct(halves.shape[1:], halves.dtype),
        in_specs=[pl.BlockSpec(memory_space=pl.ANY)],
        out_specs=pl.BlockSpec(memory_space=pl.ANY),
        scratch_shapes=[pltpu.SemaphoreType.DMA(()), pltpu.SemaphoreType.DMA(())],
        compiler_params=pltpu.CompilerParams(
            collective_id=collective_id, has_side_effects=True
        ),
    )(halves)
    own = lax.dynamic_index_in_dim(halves, lax.axis_index("core"), 0, keepdims=False)
    return (own.astype(jnp.float32) + received.astype(jnp.float32)).astype(jnp.bfloat16)


def in_stage_order(values, order):
    sizes = [lax.axis_size(a) for a in AXES]
    group = values.shape[1] // (sizes[0] * sizes[1] * sizes[2] * sizes[3])
    grid = values.reshape([values.shape[0]] + sizes + [group])
    grid = grid.transpose([0] + [1 + AXES.index(a) for a in order] + [5])
    return grid.reshape(values.shape)


def scatter_packed(pieces, order=("core", "x", "z", "y"), direct=False, collective_id=0):
    widths = [p.shape[1] for p in pieces]
    packed = jnp.concatenate(pieces, axis=1).astype(jnp.bfloat16)
    sizes = [lax.axis_size(a) for a in AXES]
    count = sizes[0] * sizes[1] * sizes[2] * sizes[3]
    per = packed.shape[0] // count
    blocks = packed
    for axis in order:
        if axis == "core":
            blocks = pair_exchange(blocks, collective_id)
        elif direct:
            size = lax.axis_size(axis)
            got = lax.all_to_all(blocks, axis, 0, 0, tiled=True)
            got = got.reshape(size, got.shape[0] // size, got.shape[1])
            blocks = jnp.sum(got.astype(jnp.float32), axis=0).astype(jnp.bfloat16)
        else:
            blocks = lax.psum_scatter(blocks, axis, scatter_dimension=0, tiled=True)
    mine = lax.optimization_barrier(blocks).astype(jnp.float32)
    out, at = [], 0
    for w in widths:
        out.append(mine[:, at : at + w])
        at += w
    return out


def per_device(
    hidden_in,
    norm1_gain,
    in_weight,
    conv_weight,
    out_weight,
    norm2_gain,
    gate_weight,
    up_weight,
    down_weight,
    segment_ids,
    cotangent,
):
    rows = hidden_in.shape[0]
    width = hidden_in.shape[1]
    per = in_weight.shape[0]
    n = lax.axis_size(AXES)
    down_rows = down_weight.shape[0]
    small = jnp.concatenate(
        [norm1_gain[:, None], norm2_gain[:, None], conv_weight], axis=1
    )
    n_small = small.shape[1]
    w_in, w_out, small_full, w_gate, w_up, w_down_packed = gather_packed(
        [
            in_weight,
            out_weight,
            pad_cols(small),
            gate_weight,
            up_weight,
            down_weight.reshape(per, -1),
        ]
    )
    w_down = w_down_packed.reshape(n * down_rows, width)
    gain1 = small_full[:, 0]
    gain2 = small_full[:, 1]
    w_conv = small_full[:, 2 : 2 + CONV]

    xf = hidden_in.astype(jnp.float32)
    s1 = rms_scale(xf)
    h = (xf * s1 * gain1.astype(jnp.float32)).astype(jnp.bfloat16)
    proj = jnp.dot(h, w_in, preferred_element_type=jnp.float32)
    bgate = proj[:, :width]
    cgate = proj[:, width : 2 * width]
    xv = proj[:, 2 * width :]
    bx = (bgate * xv).astype(jnp.bfloat16)
    prev_rows, prev_ids = shifted(
        (bx[rows - 2 :], segment_ids[rows - 2 :].astype(jnp.bfloat16)), AXES, 1
    )
    ext_bx = jnp.concatenate([prev_rows, bx], axis=0).astype(jnp.float32)
    ext_ids = jnp.concatenate([prev_ids.astype(jnp.int32), segment_ids], axis=0)
    taps = w_conv.astype(jnp.float32)
    masks = [
        (ext_ids[2 - k : 2 - k + rows] == segment_ids).astype(jnp.float32)[:, None]
        for k in range(CONV)
    ]
    conv_out = jnp.zeros((rows, width), jnp.float32)
    for k in range(CONV):
        conv_out = conv_out + taps[:, k] * masks[k] * ext_bx[2 - k : 2 - k + rows]
    y = (cgate * conv_out).astype(jnp.bfloat16)
    resid = xf + jnp.dot(y, w_out, preferred_element_type=jnp.float32)
    s2 = rms_scale(resid)
    gain2f = gain2.astype(jnp.float32)
    h2 = (resid * s2 * gain2f).astype(jnp.bfloat16)
    a = jnp.dot(h2, w_gate, preferred_element_type=jnp.float32)
    b = jnp.dot(h2, w_up, preferred_element_type=jnp.float32)
    sig = jax.nn.sigmoid(a)
    act = a * sig
    z = (act * b).astype(jnp.bfloat16)
    block_out = (resid + jnp.dot(z, w_down, preferred_element_type=jnp.float32)).astype(
        jnp.bfloat16
    )

    dz = lax.dot_general(
        cotangent, w_down, (((1,), (1,)), ((), ())), preferred_element_type=jnp.float32
    )
    da = (dz * b * sig * (1.0 + a * (1.0 - sig))).astype(jnp.bfloat16)
    db = (dz * act).astype(jnp.bfloat16)
    h2_up = in_stage_order(h2, ORDER_UP)
    g_down = lax.dot_general(
        in_stage_order(z, ORDER_DOWN),
        cotangent,
        (((0,), (0,)), ((), ())),
        preferred_element_type=jnp.bfloat16,
    )
    g_gate = lax.dot_general(
        h2_up, da, (((0,), (0,)), ((), ())), preferred_element_type=jnp.bfloat16
    )
    g_up = lax.dot_general(
        h2_up, db, (((0,), (0,)), ((), ())), preferred_element_type=jnp.bfloat16
    )
    own_gate, own_up = scatter_packed([g_gate, g_up], order=ORDER_UP)
    (own_down,) = scatter_packed(
        [g_down],
        order=ORDER_DOWN,
        direct=True,
        collective_id=1,
    )
    dh2 = lax.dot_general(da, w_gate, (((1,), (1,)), ((), ())), preferred_element_type=jnp.float32)
    dh2 = dh2 + lax.dot_general(
        db, w_up, (((1,), (1,)), ((), ())), preferred_element_type=jnp.float32
    )
    g_gain2 = jnp.sum(dh2 * resid * s2, axis=0)
    dn2 = dh2 * gain2f
    d_resid = (
        cotangent.astype(jnp.float32)
        + s2 * dn2
        - resid * (s2 * s2 * s2) * jnp.mean(dn2 * resid, axis=-1, keepdims=True)
    )
    d_out = d_resid.astype(jnp.bfloat16)
    g_out = lax.dot_general(
        in_stage_order(y, ORDER_IN),
        d_out,
        (((0,), (0,)), ((), ())),
        preferred_element_type=jnp.bfloat16,
    )
    dy = lax.dot_general(d_out, w_out, (((1,), (1,)), ((), ())), preferred_element_type=jnp.float32)
    d_cgate = dy * conv_out
    d_conv = dy * cgate
    d_ext = jnp.zeros((rows + 2, width), jnp.float32)
    tap_cols = []
    for k in range(CONV):
        term = d_conv * masks[k]
        d_ext = d_ext + jnp.pad(taps[:, k] * term, ((2 - k, k), (0, 0)))
        tap_cols.append(jnp.sum(term * ext_bx[2 - k : 2 - k + rows], axis=0))
    g_conv = jnp.stack(tap_cols, axis=1)
    returned = shifted(d_ext[:2], AXES, -1)
    d_bx = d_ext[2:] + jnp.pad(returned, ((rows - 2, 0), (0, 0)))
    d_proj = jnp.concatenate([d_bx * xv, d_cgate, d_bx * bgate], axis=1).astype(jnp.bfloat16)
    g_in = lax.dot_general(
        in_stage_order(h, ORDER_IN),
        d_proj,
        (((0,), (0,)), ((), ())),
        preferred_element_type=jnp.bfloat16,
    )
    dh = lax.dot_general(d_proj, w_in, (((1,), (1,)), ((), ())), preferred_element_type=jnp.float32)
    g_gain1 = jnp.sum(dh * xf * s1, axis=0)
    dn1 = dh * gain1.astype(jnp.float32)
    input_grad = (
        d_resid + s1 * dn1 - xf * (s1 * s1 * s1) * jnp.mean(dn1 * xf, axis=-1, keepdims=True)
    )
    g_small = jnp.concatenate([g_gain1[:, None], g_gain2[:, None], g_conv], axis=1)
    own_in, own_out = scatter_packed(
        [g_in, g_out], order=ORDER_IN, direct=True, collective_id=2
    )
    (own_small,) = exchange_packed([pad_cols(g_small)])
    return (
        block_out,
        input_grad,
        own_small[:, 0],
        own_in,
        own_small[:, 2 : 2 + CONV],
        own_out,
        own_small[:, 1],
        own_gate,
        own_up,
        own_down.reshape(down_rows, width),
    )


def solution(mesh):
    torus = jax.sharding.Mesh(mesh.devices.reshape(4, 4, 4, 2), AXES)
    return jax.shard_map(
        per_device,
        mesh=torus,
        in_specs=(
            P(FSDP, None),
            P(FSDP),
            P(FSDP, None),
            P(FSDP, None),
            P(FSDP, None),
            P(FSDP),
            P(FSDP, None),
            P(FSDP, None),
            P(FSDP, None),
            P(FSDP),
            P(FSDP, None),
        ),
        out_specs=(
            P(FSDP, None),
            P(FSDP, None),
            P(FSDP),
            P(FSDP, None),
            P(FSDP, None),
            P(FSDP, None),
            P(FSDP),
            P(FSDP, None),
            P(FSDP, None),
            P(FSDP, None),
        ),
        check_vma=False,
    )
```

```python
import jax
import jax.numpy as jnp
from jax import lax
from jax.experimental import pallas as pl
from jax.experimental.pallas import tpu as pltpu
from jax.sharding import PartitionSpec as P

CONV = 3
EPS = 1e-05
LANE = 256


def shifted(value, axis, by):
    size = lax.axis_size(axis)
    pairs = [(i, i + by) for i in range(size) if 0 <= i + by < size]
    return lax.ppermute(value, axis, pairs)


def rms_scale(values):
    return lax.rsqrt(jnp.mean(values * values, axis=-1, keepdims=True) + EPS)


def pad_cols(x):
    extra = (-x.shape[1]) % LANE
    return jnp.pad(x, ((0, 0), (0, extra))) if extra else x


def gather_packed(pieces):
    widths = [p.shape[1] for p in pieces]
    packed = jnp.concatenate(pieces, axis=1)
    full = lax.all_gather(packed, AXES, axis=0, tiled=True)
    out, at = [], 0
    for w in widths:
        out.append(full[:, at : at + w])
        at += w
    return out


AXES = ("y", "z", "x", "core")
FSDP = AXES
ORDER_UP = ("core", "x", "z", "y")
ORDER_DOWN = ("core", "z", "y", "x")
ORDER_IN = ("core", "y", "x", "z")


def exchange_packed(pieces, dtype=jnp.float32):
    widths = [p.shape[1] for p in pieces]
    packed = jnp.concatenate(pieces, axis=1)
    n = lax.axis_size(AXES)
    blocks = lax.all_to_all(packed.astype(dtype), AXES, 0, 0, tiled=True)
    blocks = blocks.reshape(n, blocks.shape[0] // n, blocks.shape[1])
    mine = lax.optimization_barrier(jnp.sum(blocks.astype(jnp.float32), axis=0))
    out, at = [], 0
    for w in widths:
        out.append(mine[:, at : at + w])
        at += w
    return out


def pair_kernel(x_ref, o_ref, send_sem, recv_sem):
    other = 1 - lax.axis_index("core")
    partner = (lax.axis_index("y"), lax.axis_index("z"), lax.axis_index("x"), other)
    barrier = pltpu.get_barrier_semaphore()
    pl.semaphore_signal(
        barrier, inc=1, device_id=partner, device_id_type=pl.DeviceIdType.MESH
    )
    pl.semaphore_wait(barrier, 1)
    copy = pltpu.make_async_remote_copy(
        src_ref=x_ref.at[other],
        dst_ref=o_ref,
        send_sem=send_sem,
        recv_sem=recv_sem,
        device_id=partner,
        device_id_type=pl.DeviceIdType.MESH,
    )
    copy.start()
    copy.wait()


def pair_exchange(blocks, collective_id):
    halves = blocks.reshape(2, blocks.shape[0] // 2, blocks.shape[1])
    received = pl.pallas_call(
        pair_kernel,
        out_shape=jax.ShapeDtypeStruct(halves.shape[1:], halves.dtype),
        in_specs=[pl.BlockSpec(memory_space=pl.ANY)],
        out_specs=pl.BlockSpec(memory_space=pl.ANY),
        scratch_shapes=[pltpu.SemaphoreType.DMA(()), pltpu.SemaphoreType.DMA(())],
        compiler_params=pltpu.CompilerParams(
            collective_id=collective_id, has_side_effects=True
        ),
    )(halves)
    own = lax.dynamic_index_in_dim(halves, lax.axis_index("core"), 0, keepdims=False)
    return (own.astype(jnp.float32) + received.astype(jnp.float32)).astype(jnp.bfloat16)


def in_stage_order(values, order):
    sizes = [lax.axis_size(a) for a in AXES]
    group = values.shape[1] // (sizes[0] * sizes[1] * sizes[2] * sizes[3])
    grid = values.reshape([values.shape[0]] + sizes + [group])
    grid = grid.transpose([0] + [1 + AXES.index(a) for a in order] + [5])
    return grid.reshape(values.shape)


def scatter_packed(pieces, order=("core", "x", "z", "y"), direct=False, collective_id=0):
    widths = [p.shape[1] for p in pieces]
    packed = jnp.concatenate(pieces, axis=1).astype(jnp.bfloat16)
    sizes = [lax.axis_size(a) for a in AXES]
    count = sizes[0] * sizes[1] * sizes[2] * sizes[3]
    per = packed.shape[0] // count
    blocks = packed
    for axis in order:
        if axis == "core":
            blocks = pair_exchange(blocks, collective_id)
        elif direct:
            size = lax.axis_size(axis)
            got = lax.all_to_all(blocks, axis, 0, 0, tiled=True)
            got = got.reshape(size, got.shape[0] // size, got.shape[1])
            blocks = jnp.sum(got.astype(jnp.float32), axis=0).astype(jnp.bfloat16)
        else:
            blocks = lax.psum_scatter(blocks, axis, scatter_dimension=0, tiled=True)
    mine = lax.optimization_barrier(blocks).astype(jnp.float32)
    out, at = [], 0
    for w in widths:
        out.append(mine[:, at : at + w])
        at += w
    return out


def per_device(
    hidden_in,
    norm1_gain,
    in_weight,
    conv_weight,
    out_weight,
    norm2_gain,
    gate_weight,
    up_weight,
    down_weight,
    segment_ids,
    cotangent,
):
    rows = hidden_in.shape[0]
    width = hidden_in.shape[1]
    per = in_weight.shape[0]
    n = lax.axis_size(AXES)
    down_rows = down_weight.shape[0]
    small = jnp.concatenate(
        [norm1_gain[:, None], norm2_gain[:, None], conv_weight], axis=1
    )
    n_small = small.shape[1]
    w_in, w_out, small_full, w_gate, w_up, w_down_packed = gather_packed(
        [
            in_weight,
            out_weight,
            pad_cols(small),
            gate_weight,
            up_weight,
            down_weight.reshape(per, -1),
        ]
    )
    w_down = w_down_packed.reshape(n * down_rows, width)
    gain1 = small_full[:, 0]
    gain2 = small_full[:, 1]
    w_conv = small_full[:, 2 : 2 + CONV]

    xf = hidden_in.astype(jnp.float32)
    s1 = rms_scale(xf)
    h = (xf * s1 * gain1.astype(jnp.float32)).astype(jnp.bfloat16)
    proj = jnp.dot(h, w_in, preferred_element_type=jnp.float32)
    bgate = proj[:, :width]
    cgate = proj[:, width : 2 * width]
    xv = proj[:, 2 * width :]
    bx = (bgate * xv).astype(jnp.bfloat16)
    prev_rows, prev_ids = shifted(
        (bx[rows - 2 :], segment_ids[rows - 2 :].astype(jnp.bfloat16)), AXES, 1
    )
    ext_bx = jnp.concatenate([prev_rows, bx], axis=0).astype(jnp.float32)
    ext_ids = jnp.concatenate([prev_ids.astype(jnp.int32), segment_ids], axis=0)
    taps = w_conv.astype(jnp.float32)
    masks = [
        (ext_ids[2 - k : 2 - k + rows] == segment_ids).astype(jnp.float32)[:, None]
        for k in range(CONV)
    ]
    conv_out = jnp.zeros((rows, width), jnp.float32)
    for k in range(CONV):
        conv_out = conv_out + taps[:, k] * masks[k] * ext_bx[2 - k : 2 - k + rows]
    y = (cgate * conv_out).astype(jnp.bfloat16)
    resid = xf + jnp.dot(y, w_out, preferred_element_type=jnp.float32)
    s2 = rms_scale(resid)
    gain2f = gain2.astype(jnp.float32)
    h2 = (resid * s2 * gain2f).astype(jnp.bfloat16)
    a = jnp.dot(h2, w_gate, preferred_element_type=jnp.float32)
    b = jnp.dot(h2, w_up, preferred_element_type=jnp.float32)
    sig = jax.nn.sigmoid(a)
    act = a * sig
    z = (act * b).astype(jnp.bfloat16)
    block_out = (resid + jnp.dot(z, w_down, preferred_element_type=jnp.float32)).astype(
        jnp.bfloat16
    )

    dz = lax.dot_general(
        cotangent, w_down, (((1,), (1,)), ((), ())), preferred_element_type=jnp.float32
    )
    da = (dz * b * sig * (1.0 + a * (1.0 - sig))).astype(jnp.bfloat16)
    db = (dz * act).astype(jnp.bfloat16)
    h2_up = in_stage_order(h2, ORDER_UP)
    g_down = lax.dot_general(
        in_stage_order(z, ORDER_DOWN),
        cotangent,
        (((0,), (0,)), ((), ())),
        preferred_element_type=jnp.bfloat16,
    )
    g_gate_up = lax.dot_general(
        h2_up,
        jnp.concatenate([da, db], axis=1),
        (((0,), (0,)), ((), ())),
        preferred_element_type=jnp.bfloat16,
    )
    (own_gate_up,) = scatter_packed([g_gate_up], order=ORDER_UP)
    own_gate = own_gate_up[:, : da.shape[1]]
    own_up = own_gate_up[:, da.shape[1] :]
    (own_down,) = scatter_packed(
        [g_down],
        order=ORDER_DOWN,
        direct=True,
        collective_id=1,
    )
    dh2 = lax.dot_general(da, w_gate, (((1,), (1,)), ((), ())), preferred_element_type=jnp.float32)
    dh2 = dh2 + lax.dot_general(
        db, w_up, (((1,), (1,)), ((), ())), preferred_element_type=jnp.float32
    )
    g_gain2 = jnp.sum(dh2 * resid * s2, axis=0)
    dn2 = dh2 * gain2f
    d_resid = (
        cotangent.astype(jnp.float32)
        + s2 * dn2
        - resid * (s2 * s2 * s2) * jnp.mean(dn2 * resid, axis=-1, keepdims=True)
    )
    d_out = d_resid.astype(jnp.bfloat16)
    g_out = lax.dot_general(
        in_stage_order(y, ORDER_IN),
        d_out,
        (((0,), (0,)), ((), ())),
        preferred_element_type=jnp.bfloat16,
    )
    dy = lax.dot_general(d_out, w_out, (((1,), (1,)), ((), ())), preferred_element_type=jnp.float32)
    d_cgate = dy * conv_out
    d_conv = dy * cgate
    d_ext = jnp.zeros((rows + 2, width), jnp.float32)
    tap_cols = []
    for k in range(CONV):
        term = d_conv * masks[k]
        d_ext = d_ext + jnp.pad(taps[:, k] * term, ((2 - k, k), (0, 0)))
        tap_cols.append(jnp.sum(term * ext_bx[2 - k : 2 - k + rows], axis=0))
    g_conv = jnp.stack(tap_cols, axis=1)
    returned = shifted(d_ext[:2], AXES, -1)
    d_bx = d_ext[2:] + jnp.pad(returned, ((rows - 2, 0), (0, 0)))
    d_proj = jnp.concatenate([d_bx * xv, d_cgate, d_bx * bgate], axis=1).astype(jnp.bfloat16)
    g_in = lax.dot_general(
        in_stage_order(h, ORDER_IN),
        d_proj,
        (((0,), (0,)), ((), ())),
        preferred_element_type=jnp.bfloat16,
    )
    dh = lax.dot_general(d_proj, w_in, (((1,), (1,)), ((), ())), preferred_element_type=jnp.float32)
    g_gain1 = jnp.sum(dh * xf * s1, axis=0)
    dn1 = dh * gain1.astype(jnp.float32)
    input_grad = (
        d_resid + s1 * dn1 - xf * (s1 * s1 * s1) * jnp.mean(dn1 * xf, axis=-1, keepdims=True)
    )
    g_small = jnp.concatenate([g_gain1[:, None], g_gain2[:, None], g_conv], axis=1)
    own_in, own_out = scatter_packed(
        [g_in, g_out], order=ORDER_IN, direct=True, collective_id=2
    )
    (own_small,) = exchange_packed([pad_cols(g_small)])
    return (
        block_out,
        input_grad,
        own_small[:, 0],
        own_in,
        own_small[:, 2 : 2 + CONV],
        own_out,
        own_small[:, 1],
        own_gate,
        own_up,
        own_down.reshape(down_rows, width),
    )


def solution(mesh):
    torus = jax.sharding.Mesh(mesh.devices.reshape(4, 4, 4, 2), AXES)
    return jax.shard_map(
        per_device,
        mesh=torus,
        in_specs=(
            P(FSDP, None),
            P(FSDP),
            P(FSDP, None),
            P(FSDP, None),
            P(FSDP, None),
            P(FSDP),
            P(FSDP, None),
            P(FSDP, None),
            P(FSDP, None),
            P(FSDP),
            P(FSDP, None),
        ),
        out_specs=(
            P(FSDP, None),
            P(FSDP, None),
            P(FSDP),
            P(FSDP, None),
            P(FSDP, None),
            P(FSDP, None),
            P(FSDP),
            P(FSDP, None),
            P(FSDP, None),
            P(FSDP, None),
        ),
        check_vma=False,
    )
```

```python
import jax
import jax.numpy as jnp
from jax import lax
from jax.experimental import pallas as pl
from jax.experimental.pallas import tpu as pltpu
from jax.sharding import PartitionSpec as P

CONV = 3
EPS = 1e-05
LANE = 256


def shifted(value, axis, by):
    size = lax.axis_size(axis)
    pairs = [(i, i + by) for i in range(size) if 0 <= i + by < size]
    return lax.ppermute(value, axis, pairs)


def rms_scale(values):
    return lax.rsqrt(jnp.mean(values * values, axis=-1, keepdims=True) + EPS)


def pad_cols(x):
    extra = (-x.shape[1]) % LANE
    return jnp.pad(x, ((0, 0), (0, extra))) if extra else x


def gather_packed(pieces):
    widths = [p.shape[1] for p in pieces]
    packed = jnp.concatenate(pieces, axis=1)
    full = lax.all_gather(packed, AXES, axis=0, tiled=True)
    out, at = [], 0
    for w in widths:
        out.append(full[:, at : at + w])
        at += w
    return out


AXES = ("y", "z", "x", "core")
FSDP = AXES
ORDER_UP = ("core", "x", "z", "y")
ORDER_DOWN = ("core", "z", "y", "x")
ORDER_IN = ("core", "y", "x", "z")


def exchange_packed(pieces, dtype=jnp.float32):
    widths = [p.shape[1] for p in pieces]
    packed = jnp.concatenate(pieces, axis=1)
    n = lax.axis_size(AXES)
    blocks = lax.all_to_all(packed.astype(dtype), AXES, 0, 0, tiled=True)
    blocks = blocks.reshape(n, blocks.shape[0] // n, blocks.shape[1])
    mine = lax.optimization_barrier(jnp.sum(blocks.astype(jnp.float32), axis=0))
    out, at = [], 0
    for w in widths:
        out.append(mine[:, at : at + w])
        at += w
    return out


def pair_kernel(x_ref, o_ref, send_sem, recv_sem):
    other = 1 - lax.axis_index("core")
    partner = (lax.axis_index("y"), lax.axis_index("z"), lax.axis_index("x"), other)
    barrier = pltpu.get_barrier_semaphore()
    pl.semaphore_signal(
        barrier, inc=1, device_id=partner, device_id_type=pl.DeviceIdType.MESH
    )
    pl.semaphore_wait(barrier, 1)
    copy = pltpu.make_async_remote_copy(
        src_ref=x_ref.at[other],
        dst_ref=o_ref,
        send_sem=send_sem,
        recv_sem=recv_sem,
        device_id=partner,
        device_id_type=pl.DeviceIdType.MESH,
    )
    copy.start()
    copy.wait()


def pair_exchange(blocks, collective_id, dtype=jnp.bfloat16):
    halves = blocks.reshape(2, blocks.shape[0] // 2, blocks.shape[1])
    received = pl.pallas_call(
        pair_kernel,
        out_shape=jax.ShapeDtypeStruct(halves.shape[1:], halves.dtype),
        in_specs=[pl.BlockSpec(memory_space=pl.ANY)],
        out_specs=pl.BlockSpec(memory_space=pl.ANY),
        scratch_shapes=[pltpu.SemaphoreType.DMA(()), pltpu.SemaphoreType.DMA(())],
        compiler_params=pltpu.CompilerParams(
            collective_id=collective_id, has_side_effects=True
        ),
    )(halves)
    own = lax.dynamic_index_in_dim(halves, lax.axis_index("core"), 0, keepdims=False)
    return (own.astype(jnp.float32) + received.astype(jnp.float32)).astype(dtype)


def in_stage_order(values, order):
    sizes = [lax.axis_size(a) for a in AXES]
    group = values.shape[1] // (sizes[0] * sizes[1] * sizes[2] * sizes[3])
    grid = values.reshape([values.shape[0]] + sizes + [group])
    grid = grid.transpose([0] + [1 + AXES.index(a) for a in order] + [5])
    return grid.reshape(values.shape)


def scatter_packed(
    pieces, order=("core", "x", "z", "y"), direct=False, collective_id=0, dtype=jnp.bfloat16
):
    widths = [p.shape[1] for p in pieces]
    packed = jnp.concatenate(pieces, axis=1).astype(dtype)
    sizes = [lax.axis_size(a) for a in AXES]
    count = sizes[0] * sizes[1] * sizes[2] * sizes[3]
    per = packed.shape[0] // count
    blocks = packed
    for axis in order:
        if axis == "core":
            blocks = pair_exchange(blocks, collective_id, dtype)
        elif direct:
            size = lax.axis_size(axis)
            got = lax.all_to_all(blocks, axis, 0, 0, tiled=True)
            got = got.reshape(size, got.shape[0] // size, got.shape[1])
            blocks = jnp.sum(got.astype(jnp.float32), axis=0).astype(dtype)
        else:
            blocks = lax.psum_scatter(blocks, axis, scatter_dimension=0, tiled=True)
    mine = lax.optimization_barrier(blocks).astype(jnp.float32)
    out, at = [], 0
    for w in widths:
        out.append(mine[:, at : at + w])
        at += w
    return out


def per_device(
    hidden_in,
    norm1_gain,
    in_weight,
    conv_weight,
    out_weight,
    norm2_gain,
    gate_weight,
    up_weight,
    down_weight,
    segment_ids,
    cotangent,
):
    rows = hidden_in.shape[0]
    width = hidden_in.shape[1]
    per = in_weight.shape[0]
    n = lax.axis_size(AXES)
    down_rows = down_weight.shape[0]
    small = jnp.concatenate(
        [norm1_gain[:, None], norm2_gain[:, None], conv_weight], axis=1
    )
    n_small = small.shape[1]
    w_in, w_out, small_full, w_gate, w_up, w_down_packed = gather_packed(
        [
            in_weight,
            out_weight,
            pad_cols(small),
            gate_weight,
            up_weight,
            down_weight.reshape(per, -1),
        ]
    )
    w_down = w_down_packed.reshape(n * down_rows, width)
    gain1 = small_full[:, 0]
    gain2 = small_full[:, 1]
    w_conv = small_full[:, 2 : 2 + CONV]

    xf = hidden_in.astype(jnp.float32)
    s1 = rms_scale(xf)
    h = (xf * s1 * gain1.astype(jnp.float32)).astype(jnp.bfloat16)
    proj = jnp.dot(h, w_in, preferred_element_type=jnp.float32)
    bgate = proj[:, :width]
    cgate = proj[:, width : 2 * width]
    xv = proj[:, 2 * width :]
    bx = (bgate * xv).astype(jnp.bfloat16)
    prev_rows, prev_ids = shifted(
        (bx[rows - 2 :], segment_ids[rows - 2 :].astype(jnp.bfloat16)), AXES, 1
    )
    ext_bx = jnp.concatenate([prev_rows, bx], axis=0).astype(jnp.float32)
    ext_ids = jnp.concatenate([prev_ids.astype(jnp.int32), segment_ids], axis=0)
    taps = w_conv.astype(jnp.float32)
    masks = [
        (ext_ids[2 - k : 2 - k + rows] == segment_ids).astype(jnp.float32)[:, None]
        for k in range(CONV)
    ]
    conv_out = jnp.zeros((rows, width), jnp.float32)
    for k in range(CONV):
        conv_out = conv_out + taps[:, k] * masks[k] * ext_bx[2 - k : 2 - k + rows]
    y = (cgate * conv_out).astype(jnp.bfloat16)
    resid = xf + jnp.dot(y, w_out, preferred_element_type=jnp.float32)
    s2 = rms_scale(resid)
    gain2f = gain2.astype(jnp.float32)
    h2 = (resid * s2 * gain2f).astype(jnp.bfloat16)
    a = jnp.dot(h2, w_gate, preferred_element_type=jnp.float32)
    b = jnp.dot(h2, w_up, preferred_element_type=jnp.float32)
    sig = jax.nn.sigmoid(a)
    act = a * sig
    z = (act * b).astype(jnp.bfloat16)
    block_out = (resid + jnp.dot(z, w_down, preferred_element_type=jnp.float32)).astype(
        jnp.bfloat16
    )

    dz = lax.dot_general(
        cotangent, w_down, (((1,), (1,)), ((), ())), preferred_element_type=jnp.float32
    )
    da = (dz * b * sig * (1.0 + a * (1.0 - sig))).astype(jnp.bfloat16)
    db = (dz * act).astype(jnp.bfloat16)
    h2_up = in_stage_order(h2, ORDER_UP)
    g_down = lax.dot_general(
        in_stage_order(z, ORDER_DOWN),
        cotangent,
        (((0,), (0,)), ((), ())),
        preferred_element_type=jnp.bfloat16,
    )
    g_gate = lax.dot_general(
        h2_up, da, (((0,), (0,)), ((), ())), preferred_element_type=jnp.bfloat16
    )
    g_up = lax.dot_general(
        h2_up, db, (((0,), (0,)), ((), ())), preferred_element_type=jnp.bfloat16
    )
    own_gate, own_up = scatter_packed([g_gate, g_up], order=ORDER_UP)
    (own_down,) = scatter_packed(
        [g_down],
        order=ORDER_DOWN,
        direct=True,
        collective_id=1,
    )
    dh2 = lax.dot_general(da, w_gate, (((1,), (1,)), ((), ())), preferred_element_type=jnp.float32)
    dh2 = dh2 + lax.dot_general(
        db, w_up, (((1,), (1,)), ((), ())), preferred_element_type=jnp.float32
    )
    g_gain2 = jnp.sum(dh2 * resid * s2, axis=0)
    dn2 = dh2 * gain2f
    d_resid = (
        cotangent.astype(jnp.float32)
        + s2 * dn2
        - resid * (s2 * s2 * s2) * jnp.mean(dn2 * resid, axis=-1, keepdims=True)
    )
    d_out = d_resid.astype(jnp.bfloat16)
    g_out = lax.dot_general(
        in_stage_order(y, ORDER_IN),
        d_out,
        (((0,), (0,)), ((), ())),
        preferred_element_type=jnp.bfloat16,
    )
    dy = lax.dot_general(d_out, w_out, (((1,), (1,)), ((), ())), preferred_element_type=jnp.float32)
    d_cgate = dy * conv_out
    d_conv = dy * cgate
    d_ext = jnp.zeros((rows + 2, width), jnp.float32)
    tap_cols = []
    for k in range(CONV):
        term = d_conv * masks[k]
        d_ext = d_ext + jnp.pad(taps[:, k] * term, ((2 - k, k), (0, 0)))
        tap_cols.append(jnp.sum(term * ext_bx[2 - k : 2 - k + rows], axis=0))
    g_conv = jnp.stack(tap_cols, axis=1)
    returned = shifted(d_ext[:2], AXES, -1)
    d_bx = d_ext[2:] + jnp.pad(returned, ((rows - 2, 0), (0, 0)))
    d_proj = jnp.concatenate([d_bx * xv, d_cgate, d_bx * bgate], axis=1).astype(jnp.bfloat16)
    g_in = lax.dot_general(
        in_stage_order(h, ORDER_IN),
        d_proj,
        (((0,), (0,)), ((), ())),
        preferred_element_type=jnp.bfloat16,
    )
    dh = lax.dot_general(d_proj, w_in, (((1,), (1,)), ((), ())), preferred_element_type=jnp.float32)
    g_gain1 = jnp.sum(dh * xf * s1, axis=0)
    dn1 = dh * gain1.astype(jnp.float32)
    input_grad = (
        d_resid + s1 * dn1 - xf * (s1 * s1 * s1) * jnp.mean(dn1 * xf, axis=-1, keepdims=True)
    )
    g_small = jnp.concatenate([g_gain1[:, None], g_gain2[:, None], g_conv], axis=1)
    own_in, own_out = scatter_packed(
        [g_in, g_out], order=ORDER_IN, direct=True, collective_id=2
    )
    g_small = in_stage_order(g_small.T, ORDER_IN).T
    (own_small,) = scatter_packed(
        [pad_cols(g_small)],
        order=ORDER_IN,
        direct=True,
        collective_id=3,
        dtype=jnp.float32,
    )
    return (
        block_out,
        input_grad,
        own_small[:, 0],
        own_in,
        own_small[:, 2 : 2 + CONV],
        own_out,
        own_small[:, 1],
        own_gate,
        own_up,
        own_down.reshape(down_rows, width),
    )


def solution(mesh):
    torus = jax.sharding.Mesh(mesh.devices.reshape(4, 4, 4, 2), AXES)
    return jax.shard_map(
        per_device,
        mesh=torus,
        in_specs=(
            P(FSDP, None),
            P(FSDP),
            P(FSDP, None),
            P(FSDP, None),
            P(FSDP, None),
            P(FSDP),
            P(FSDP, None),
            P(FSDP, None),
            P(FSDP, None),
            P(FSDP),
            P(FSDP, None),
        ),
        out_specs=(
            P(FSDP, None),
            P(FSDP, None),
            P(FSDP),
            P(FSDP, None),
            P(FSDP, None),
            P(FSDP, None),
            P(FSDP),
            P(FSDP, None),
            P(FSDP, None),
            P(FSDP, None),
        ),
        check_vma=False,
    )
```

```python
import jax
import jax.numpy as jnp
from jax import lax
from jax.experimental import pallas as pl
from jax.experimental.pallas import tpu as pltpu
from jax.sharding import PartitionSpec as P

CONV = 3
EPS = 1e-05
LANE = 256


def shifted(value, axis, by):
    size = lax.axis_size(axis)
    pairs = [(i, i + by) for i in range(size) if 0 <= i + by < size]
    return lax.ppermute(value, axis, pairs)


def rms_scale(values):
    return lax.rsqrt(jnp.mean(values * values, axis=-1, keepdims=True) + EPS)


def pad_cols(x):
    extra = (-x.shape[1]) % LANE
    return jnp.pad(x, ((0, 0), (0, extra))) if extra else x


def gather_packed(pieces):
    widths = [p.shape[1] for p in pieces]
    packed = jnp.concatenate(pieces, axis=1)
    full = lax.all_gather(packed, AXES, axis=0, tiled=True)
    out, at = [], 0
    for w in widths:
        out.append(full[:, at : at + w])
        at += w
    return out


AXES = ("y", "z", "x", "core")
FSDP = AXES
ORDER_UP = ("core", "x", "z", "y")
ORDER_DOWN = ("core", "y", "z", "x")
ORDER_IN = ("core", "y", "x", "z")


def exchange_packed(pieces, dtype=jnp.float32):
    widths = [p.shape[1] for p in pieces]
    packed = jnp.concatenate(pieces, axis=1)
    n = lax.axis_size(AXES)
    blocks = lax.all_to_all(packed.astype(dtype), AXES, 0, 0, tiled=True)
    blocks = blocks.reshape(n, blocks.shape[0] // n, blocks.shape[1])
    mine = lax.optimization_barrier(jnp.sum(blocks.astype(jnp.float32), axis=0))
    out, at = [], 0
    for w in widths:
        out.append(mine[:, at : at + w])
        at += w
    return out


def pair_kernel(x_ref, o_ref, send_sem, recv_sem):
    other = 1 - lax.axis_index("core")
    partner = (lax.axis_index("y"), lax.axis_index("z"), lax.axis_index("x"), other)
    barrier = pltpu.get_barrier_semaphore()
    pl.semaphore_signal(
        barrier, inc=1, device_id=partner, device_id_type=pl.DeviceIdType.MESH
    )
    pl.semaphore_wait(barrier, 1)
    copy = pltpu.make_async_remote_copy(
        src_ref=x_ref.at[other],
        dst_ref=o_ref,
        send_sem=send_sem,
        recv_sem=recv_sem,
        device_id=partner,
        device_id_type=pl.DeviceIdType.MESH,
    )
    copy.start()
    copy.wait()


def pair_exchange(blocks, collective_id):
    halves = blocks.reshape(2, blocks.shape[0] // 2, blocks.shape[1])
    received = pl.pallas_call(
        pair_kernel,
        out_shape=jax.ShapeDtypeStruct(halves.shape[1:], halves.dtype),
        in_specs=[pl.BlockSpec(memory_space=pl.ANY)],
        out_specs=pl.BlockSpec(memory_space=pl.ANY),
        scratch_shapes=[pltpu.SemaphoreType.DMA(()), pltpu.SemaphoreType.DMA(())],
        compiler_params=pltpu.CompilerParams(
            collective_id=collective_id, has_side_effects=True
        ),
    )(halves)
    own = lax.dynamic_index_in_dim(halves, lax.axis_index("core"), 0, keepdims=False)
    return (own.astype(jnp.float32) + received.astype(jnp.float32)).astype(jnp.bfloat16)


def in_stage_order(values, order):
    sizes = [lax.axis_size(a) for a in AXES]
    group = values.shape[1] // (sizes[0] * sizes[1] * sizes[2] * sizes[3])
    grid = values.reshape([values.shape[0]] + sizes + [group])
    grid = grid.transpose([0] + [1 + AXES.index(a) for a in order] + [5])
    return grid.reshape(values.shape)


def scatter_packed(pieces, order=("core", "x", "z", "y"), direct=False, collective_id=0):
    widths = [p.shape[1] for p in pieces]
    packed = jnp.concatenate(pieces, axis=1).astype(jnp.bfloat16)
    sizes = [lax.axis_size(a) for a in AXES]
    count = sizes[0] * sizes[1] * sizes[2] * sizes[3]
    per = packed.shape[0] // count
    blocks = packed
    for axis in order:
        if axis == "core":
            blocks = pair_exchange(blocks, collective_id)
        elif direct:
            size = lax.axis_size(axis)
            got = lax.all_to_all(blocks, axis, 0, 0, tiled=True)
            got = got.reshape(size, got.shape[0] // size, got.shape[1])
            blocks = jnp.sum(got.astype(jnp.float32), axis=0).astype(jnp.bfloat16)
        else:
            blocks = lax.psum_scatter(blocks, axis, scatter_dimension=0, tiled=True)
    mine = lax.optimization_barrier(blocks).astype(jnp.float32)
    out, at = [], 0
    for w in widths:
        out.append(mine[:, at : at + w])
        at += w
    return out


def per_device(
    hidden_in,
    norm1_gain,
    in_weight,
    conv_weight,
    out_weight,
    norm2_gain,
    gate_weight,
    up_weight,
    down_weight,
    segment_ids,
    cotangent,
):
    rows = hidden_in.shape[0]
    width = hidden_in.shape[1]
    per = in_weight.shape[0]
    n = lax.axis_size(AXES)
    down_rows = down_weight.shape[0]
    small = jnp.concatenate(
        [norm1_gain[:, None], norm2_gain[:, None], conv_weight], axis=1
    )
    n_small = small.shape[1]
    w_in, w_out, small_full, w_gate, w_up, w_down_packed = gather_packed(
        [
            in_weight,
            out_weight,
            pad_cols(small),
            gate_weight,
            up_weight,
            down_weight.reshape(per, -1),
        ]
    )
    w_down = w_down_packed.reshape(n * down_rows, width)
    gain1 = small_full[:, 0]
    gain2 = small_full[:, 1]
    w_conv = small_full[:, 2 : 2 + CONV]

    xf = hidden_in.astype(jnp.float32)
    s1 = rms_scale(xf)
    h = (xf * s1 * gain1.astype(jnp.float32)).astype(jnp.bfloat16)
    proj = jnp.dot(h, w_in, preferred_element_type=jnp.float32)
    bgate = proj[:, :width]
    cgate = proj[:, width : 2 * width]
    xv = proj[:, 2 * width :]
    bx = (bgate * xv).astype(jnp.bfloat16)
    prev_rows, prev_ids = shifted(
        (bx[rows - 2 :], segment_ids[rows - 2 :].astype(jnp.bfloat16)), AXES, 1
    )
    ext_bx = jnp.concatenate([prev_rows, bx], axis=0).astype(jnp.float32)
    ext_ids = jnp.concatenate([prev_ids.astype(jnp.int32), segment_ids], axis=0)
    taps = w_conv.astype(jnp.float32)
    masks = [
        (ext_ids[2 - k : 2 - k + rows] == segment_ids).astype(jnp.float32)[:, None]
        for k in range(CONV)
    ]
    conv_out = jnp.zeros((rows, width), jnp.float32)
    for k in range(CONV):
        conv_out = conv_out + taps[:, k] * masks[k] * ext_bx[2 - k : 2 - k + rows]
    y = (cgate * conv_out).astype(jnp.bfloat16)
    resid = xf + jnp.dot(y, w_out, preferred_element_type=jnp.float32)
    s2 = rms_scale(resid)
    gain2f = gain2.astype(jnp.float32)
    h2 = (resid * s2 * gain2f).astype(jnp.bfloat16)
    a = jnp.dot(h2, w_gate, preferred_element_type=jnp.float32)
    b = jnp.dot(h2, w_up, preferred_element_type=jnp.float32)
    sig = jax.nn.sigmoid(a)
    act = a * sig
    z = (act * b).astype(jnp.bfloat16)
    block_out = (resid + jnp.dot(z, w_down, preferred_element_type=jnp.float32)).astype(
        jnp.bfloat16
    )

    dz = lax.dot_general(
        cotangent, w_down, (((1,), (1,)), ((), ())), preferred_element_type=jnp.float32
    )
    da = (dz * b * sig * (1.0 + a * (1.0 - sig))).astype(jnp.bfloat16)
    db = (dz * act).astype(jnp.bfloat16)
    h2_up = in_stage_order(h2, ORDER_UP)
    g_down = lax.dot_general(
        in_stage_order(z, ORDER_DOWN),
        cotangent,
        (((0,), (0,)), ((), ())),
        preferred_element_type=jnp.bfloat16,
    )
    g_gate = lax.dot_general(
        h2_up, da, (((0,), (0,)), ((), ())), preferred_element_type=jnp.bfloat16
    )
    g_up = lax.dot_general(
        h2_up, db, (((0,), (0,)), ((), ())), preferred_element_type=jnp.bfloat16
    )
    own_gate, own_up = scatter_packed([g_gate, g_up], order=ORDER_UP)
    (own_down,) = scatter_packed(
        [g_down],
        order=ORDER_DOWN,
        direct=True,
        collective_id=1,
    )
    dh2 = lax.dot_general(da, w_gate, (((1,), (1,)), ((), ())), preferred_element_type=jnp.float32)
    dh2 = dh2 + lax.dot_general(
        db, w_up, (((1,), (1,)), ((), ())), preferred_element_type=jnp.float32
    )
    g_gain2 = jnp.sum(dh2 * resid * s2, axis=0)
    dn2 = dh2 * gain2f
    d_resid = (
        cotangent.astype(jnp.float32)
        + s2 * dn2
        - resid * (s2 * s2 * s2) * jnp.mean(dn2 * resid, axis=-1, keepdims=True)
    )
    d_out = d_resid.astype(jnp.bfloat16)
    g_out = lax.dot_general(
        in_stage_order(y, ORDER_IN),
        d_out,
        (((0,), (0,)), ((), ())),
        preferred_element_type=jnp.bfloat16,
    )
    dy = lax.dot_general(d_out, w_out, (((1,), (1,)), ((), ())), preferred_element_type=jnp.float32)
    d_cgate = dy * conv_out
    d_conv = dy * cgate
    d_ext = jnp.zeros((rows + 2, width), jnp.float32)
    tap_cols = []
    for k in range(CONV):
        term = d_conv * masks[k]
        d_ext = d_ext + jnp.pad(taps[:, k] * term, ((2 - k, k), (0, 0)))
        tap_cols.append(jnp.sum(term * ext_bx[2 - k : 2 - k + rows], axis=0))
    g_conv = jnp.stack(tap_cols, axis=1)
    returned = shifted(d_ext[:2], AXES, -1)
    d_bx = d_ext[2:] + jnp.pad(returned, ((rows - 2, 0), (0, 0)))
    d_proj = jnp.concatenate([d_bx * xv, d_cgate, d_bx * bgate], axis=1).astype(jnp.bfloat16)
    g_in = lax.dot_general(
        in_stage_order(h, ORDER_IN),
        d_proj,
        (((0,), (0,)), ((), ())),
        preferred_element_type=jnp.bfloat16,
    )
    dh = lax.dot_general(d_proj, w_in, (((1,), (1,)), ((), ())), preferred_element_type=jnp.float32)
    g_gain1 = jnp.sum(dh * xf * s1, axis=0)
    dn1 = dh * gain1.astype(jnp.float32)
    input_grad = (
        d_resid + s1 * dn1 - xf * (s1 * s1 * s1) * jnp.mean(dn1 * xf, axis=-1, keepdims=True)
    )
    g_small = jnp.concatenate([g_gain1[:, None], g_gain2[:, None], g_conv], axis=1)
    own_in, own_out = scatter_packed(
        [g_in, g_out], order=ORDER_IN, direct=True, collective_id=2
    )
    (own_small,) = exchange_packed([pad_cols(g_small)])
    return (
        block_out,
        input_grad,
        own_small[:, 0],
        own_in,
        own_small[:, 2 : 2 + CONV],
        own_out,
        own_small[:, 1],
        own_gate,
        own_up,
        own_down.reshape(down_rows, width),
    )


def solution(mesh):
    torus = jax.sharding.Mesh(mesh.devices.reshape(4, 4, 4, 2), AXES)
    return jax.shard_map(
        per_device,
        mesh=torus,
        in_specs=(
            P(FSDP, None),
            P(FSDP),
            P(FSDP, None),
            P(FSDP, None),
            P(FSDP, None),
            P(FSDP),
            P(FSDP, None),
            P(FSDP, None),
            P(FSDP, None),
            P(FSDP),
            P(FSDP, None),
        ),
        out_specs=(
            P(FSDP, None),
            P(FSDP, None),
            P(FSDP),
            P(FSDP, None),
            P(FSDP, None),
            P(FSDP, None),
            P(FSDP),
            P(FSDP, None),
            P(FSDP, None),
            P(FSDP, None),
        ),
        check_vma=False,
    )
```

```python
import jax
import jax.numpy as jnp
from jax import lax
from jax.experimental import pallas as pl
from jax.experimental.pallas import tpu as pltpu
from jax.sharding import PartitionSpec as P

CONV = 3
EPS = 1e-05
LANE = 256


def shifted(value, axis, by):
    size = lax.axis_size(axis)
    pairs = [(i, i + by) for i in range(size) if 0 <= i + by < size]
    return lax.ppermute(value, axis, pairs)


def rms_scale(values):
    return lax.rsqrt(jnp.mean(values * values, axis=-1, keepdims=True) + EPS)


def pad_cols(x):
    extra = (-x.shape[1]) % LANE
    return jnp.pad(x, ((0, 0), (0, extra))) if extra else x


def gather_packed(pieces):
    widths = [p.shape[1] for p in pieces]
    packed = jnp.concatenate(pieces, axis=1)
    full = lax.all_gather(packed, AXES, axis=0, tiled=True)
    out, at = [], 0
    for w in widths:
        out.append(full[:, at : at + w])
        at += w
    return out


AXES = ("y", "z", "x", "core")
FSDP = AXES
ORDER_UP = ("core", "x", "z", "y")
ORDER_DOWN = ("core", "z", "y", "x")
ORDER_IN = ("core", "y", "x", "z")


def exchange_packed(pieces, dtype=jnp.float32):
    widths = [p.shape[1] for p in pieces]
    packed = jnp.concatenate(pieces, axis=1)
    n = lax.axis_size(AXES)
    blocks = lax.all_to_all(packed.astype(dtype), AXES, 0, 0, tiled=True)
    blocks = blocks.reshape(n, blocks.shape[0] // n, blocks.shape[1])
    mine = lax.optimization_barrier(jnp.sum(blocks.astype(jnp.float32), axis=0))
    out, at = [], 0
    for w in widths:
        out.append(mine[:, at : at + w])
        at += w
    return out


def pair_kernel(x_ref, o_ref, send_sem, recv_sem):
    other = 1 - lax.axis_index("core")
    partner = (lax.axis_index("y"), lax.axis_index("z"), lax.axis_index("x"), other)
    barrier = pltpu.get_barrier_semaphore()
    pl.semaphore_signal(
        barrier, inc=1, device_id=partner, device_id_type=pl.DeviceIdType.MESH
    )
    pl.semaphore_wait(barrier, 1)
    copy = pltpu.make_async_remote_copy(
        src_ref=x_ref.at[other],
        dst_ref=o_ref,
        send_sem=send_sem,
        recv_sem=recv_sem,
        device_id=partner,
        device_id_type=pl.DeviceIdType.MESH,
    )
    copy.start()
    copy.wait()


def pair_exchange(blocks, collective_id):
    halves = blocks.reshape(2, blocks.shape[0] // 2, blocks.shape[1])
    received = pl.pallas_call(
        pair_kernel,
        out_shape=jax.ShapeDtypeStruct(halves.shape[1:], halves.dtype),
        in_specs=[pl.BlockSpec(memory_space=pl.ANY)],
        out_specs=pl.BlockSpec(memory_space=pl.ANY),
        scratch_shapes=[pltpu.SemaphoreType.DMA(()), pltpu.SemaphoreType.DMA(())],
        compiler_params=pltpu.CompilerParams(
            collective_id=collective_id, has_side_effects=True
        ),
        cost_estimate=pl.CostEstimate(
            flops=0,
            transcendentals=0,
            bytes_accessed=2 * halves[0].size * halves.dtype.itemsize,
        ),
    )(halves)
    own = lax.dynamic_index_in_dim(halves, lax.axis_index("core"), 0, keepdims=False)
    return (own.astype(jnp.float32) + received.astype(jnp.float32)).astype(jnp.bfloat16)


def in_stage_order(values, order):
    sizes = [lax.axis_size(a) for a in AXES]
    group = values.shape[1] // (sizes[0] * sizes[1] * sizes[2] * sizes[3])
    grid = values.reshape([values.shape[0]] + sizes + [group])
    grid = grid.transpose([0] + [1 + AXES.index(a) for a in order] + [5])
    return grid.reshape(values.shape)


def scatter_packed(pieces, order=("core", "x", "z", "y"), direct=False, collective_id=0):
    widths = [p.shape[1] for p in pieces]
    packed = jnp.concatenate(pieces, axis=1).astype(jnp.bfloat16)
    sizes = [lax.axis_size(a) for a in AXES]
    count = sizes[0] * sizes[1] * sizes[2] * sizes[3]
    per = packed.shape[0] // count
    blocks = packed
    for axis in order:
        if axis == "core":
            blocks = pair_exchange(blocks, collective_id)
        elif direct:
            size = lax.axis_size(axis)
            got = lax.all_to_all(blocks, axis, 0, 0, tiled=True)
            got = got.reshape(size, got.shape[0] // size, got.shape[1])
            blocks = jnp.sum(got.astype(jnp.float32), axis=0).astype(jnp.bfloat16)
        else:
            blocks = lax.psum_scatter(blocks, axis, scatter_dimension=0, tiled=True)
    mine = lax.optimization_barrier(blocks).astype(jnp.float32)
    out, at = [], 0
    for w in widths:
        out.append(mine[:, at : at + w])
        at += w
    return out


def per_device(
    hidden_in,
    norm1_gain,
    in_weight,
    conv_weight,
    out_weight,
    norm2_gain,
    gate_weight,
    up_weight,
    down_weight,
    segment_ids,
    cotangent,
):
    rows = hidden_in.shape[0]
    width = hidden_in.shape[1]
    per = in_weight.shape[0]
    n = lax.axis_size(AXES)
    down_rows = down_weight.shape[0]
    small = jnp.concatenate(
        [norm1_gain[:, None], norm2_gain[:, None], conv_weight], axis=1
    )
    n_small = small.shape[1]
    w_in, w_out, small_full, w_gate, w_up, w_down_packed = gather_packed(
        [
            in_weight,
            out_weight,
            pad_cols(small),
            gate_weight,
            up_weight,
            down_weight.reshape(per, -1),
        ]
    )
    w_down = w_down_packed.reshape(n * down_rows, width)
    gain1 = small_full[:, 0]
    gain2 = small_full[:, 1]
    w_conv = small_full[:, 2 : 2 + CONV]

    xf = hidden_in.astype(jnp.float32)
    s1 = rms_scale(xf)
    h = (xf * s1 * gain1.astype(jnp.float32)).astype(jnp.bfloat16)
    proj = jnp.dot(h, w_in, preferred_element_type=jnp.float32)
    bgate = proj[:, :width]
    cgate = proj[:, width : 2 * width]
    xv = proj[:, 2 * width :]
    bx = (bgate * xv).astype(jnp.bfloat16)
    prev_rows, prev_ids = shifted(
        (bx[rows - 2 :], segment_ids[rows - 2 :].astype(jnp.bfloat16)), AXES, 1
    )
    ext_bx = jnp.concatenate([prev_rows, bx], axis=0).astype(jnp.float32)
    ext_ids = jnp.concatenate([prev_ids.astype(jnp.int32), segment_ids], axis=0)
    taps = w_conv.astype(jnp.float32)
    masks = [
        (ext_ids[2 - k : 2 - k + rows] == segment_ids).astype(jnp.float32)[:, None]
        for k in range(CONV)
    ]
    conv_out = jnp.zeros((rows, width), jnp.float32)
    for k in range(CONV):
        conv_out = conv_out + taps[:, k] * masks[k] * ext_bx[2 - k : 2 - k + rows]
    y = (cgate * conv_out).astype(jnp.bfloat16)
    resid = xf + jnp.dot(y, w_out, preferred_element_type=jnp.float32)
    s2 = rms_scale(resid)
    gain2f = gain2.astype(jnp.float32)
    h2 = (resid * s2 * gain2f).astype(jnp.bfloat16)
    a = jnp.dot(h2, w_gate, preferred_element_type=jnp.float32)
    b = jnp.dot(h2, w_up, preferred_element_type=jnp.float32)
    sig = jax.nn.sigmoid(a)
    act = a * sig
    z = (act * b).astype(jnp.bfloat16)
    block_out = (resid + jnp.dot(z, w_down, preferred_element_type=jnp.float32)).astype(
        jnp.bfloat16
    )

    dz = lax.dot_general(
        cotangent, w_down, (((1,), (1,)), ((), ())), preferred_element_type=jnp.float32
    )
    da = (dz * b * sig * (1.0 + a * (1.0 - sig))).astype(jnp.bfloat16)
    db = (dz * act).astype(jnp.bfloat16)
    h2_up = in_stage_order(h2, ORDER_UP)
    g_down = lax.dot_general(
        in_stage_order(z, ORDER_DOWN),
        cotangent,
        (((0,), (0,)), ((), ())),
        preferred_element_type=jnp.bfloat16,
    )
    g_gate = lax.dot_general(
        h2_up, da, (((0,), (0,)), ((), ())), preferred_element_type=jnp.bfloat16
    )
    g_up = lax.dot_general(
        h2_up, db, (((0,), (0,)), ((), ())), preferred_element_type=jnp.bfloat16
    )
    own_gate, own_up = scatter_packed([g_gate, g_up], order=ORDER_UP)
    (own_down,) = scatter_packed(
        [g_down],
        order=ORDER_DOWN,
        direct=True,
        collective_id=1,
    )
    dh2 = lax.dot_general(da, w_gate, (((1,), (1,)), ((), ())), preferred_element_type=jnp.float32)
    dh2 = dh2 + lax.dot_general(
        db, w_up, (((1,), (1,)), ((), ())), preferred_element_type=jnp.float32
    )
    g_gain2 = jnp.sum(dh2 * resid * s2, axis=0)
    dn2 = dh2 * gain2f
    d_resid = (
        cotangent.astype(jnp.float32)
        + s2 * dn2
        - resid * (s2 * s2 * s2) * jnp.mean(dn2 * resid, axis=-1, keepdims=True)
    )
    d_out = d_resid.astype(jnp.bfloat16)
    g_out = lax.dot_general(
        in_stage_order(y, ORDER_IN),
        d_out,
        (((0,), (0,)), ((), ())),
        preferred_element_type=jnp.bfloat16,
    )
    dy = lax.dot_general(d_out, w_out, (((1,), (1,)), ((), ())), preferred_element_type=jnp.float32)
    d_cgate = dy * conv_out
    d_conv = dy * cgate
    d_ext = jnp.zeros((rows + 2, width), jnp.float32)
    tap_cols = []
    for k in range(CONV):
        term = d_conv * masks[k]
        d_ext = d_ext + jnp.pad(taps[:, k] * term, ((2 - k, k), (0, 0)))
        tap_cols.append(jnp.sum(term * ext_bx[2 - k : 2 - k + rows], axis=0))
    g_conv = jnp.stack(tap_cols, axis=1)
    returned = shifted(d_ext[:2], AXES, -1)
    d_bx = d_ext[2:] + jnp.pad(returned, ((rows - 2, 0), (0, 0)))
    d_proj = jnp.concatenate([d_bx * xv, d_cgate, d_bx * bgate], axis=1).astype(jnp.bfloat16)
    g_in = lax.dot_general(
        in_stage_order(h, ORDER_IN),
        d_proj,
        (((0,), (0,)), ((), ())),
        preferred_element_type=jnp.bfloat16,
    )
    dh = lax.dot_general(d_proj, w_in, (((1,), (1,)), ((), ())), preferred_element_type=jnp.float32)
    g_gain1 = jnp.sum(dh * xf * s1, axis=0)
    dn1 = dh * gain1.astype(jnp.float32)
    input_grad = (
        d_resid + s1 * dn1 - xf * (s1 * s1 * s1) * jnp.mean(dn1 * xf, axis=-1, keepdims=True)
    )
    g_small = jnp.concatenate([g_gain1[:, None], g_gain2[:, None], g_conv], axis=1)
    own_in, own_out = scatter_packed(
        [g_in, g_out], order=ORDER_IN, direct=True, collective_id=2
    )
    (own_small,) = exchange_packed([pad_cols(g_small)])
    return (
        block_out,
        input_grad,
        own_small[:, 0],
        own_in,
        own_small[:, 2 : 2 + CONV],
        own_out,
        own_small[:, 1],
        own_gate,
        own_up,
        own_down.reshape(down_rows, width),
    )


def solution(mesh):
    torus = jax.sharding.Mesh(mesh.devices.reshape(4, 4, 4, 2), AXES)
    return jax.shard_map(
        per_device,
        mesh=torus,
        in_specs=(
            P(FSDP, None),
            P(FSDP),
            P(FSDP, None),
            P(FSDP, None),
            P(FSDP, None),
            P(FSDP),
            P(FSDP, None),
            P(FSDP, None),
            P(FSDP, None),
            P(FSDP),
            P(FSDP, None),
        ),
        out_specs=(
            P(FSDP, None),
            P(FSDP, None),
            P(FSDP),
            P(FSDP, None),
            P(FSDP, None),
            P(FSDP, None),
            P(FSDP),
            P(FSDP, None),
            P(FSDP, None),
            P(FSDP, None),
        ),
        check_vma=False,
    )
```
